32 devices in a mesh: runs: 2 (over y), shot: 4 (over x, core), slab: 4 (over z).
Axes of the slice: x: 2, y: 2, z: 4, core: 2. Of those that a mesh axis runs over, the one named last changes fastest.
Arguments:
- source_now: float32 [16, 64, 16, 256], P(('runs', 'shot'), 'slab'), parts along dimension 0, may hold values from -4 to 4
- source_prev: float32 [16, 64, 16, 256], P(('runs', 'shot'), 'slab'), parts along dimension 0, may hold values from -4 to 4
- receiver_now: float32 [16, 64, 16, 256], P(('runs', 'shot'), 'slab'), parts along dimension 0, may hold values from -4 to 4
- receiver_prev: float32 [16, 64, 16, 256], P(('runs', 'shot'), 'slab'), parts along dimension 0, may hold values from -4 to 4
- courant_sq: float32 [128, 16, 256], P(('runs', 'slab')), parts along dimension 0, may hold values from 0.26 to 0.52
- source_cell: int32 [16], P(('runs', 'shot')), parts along dimension 0, may hold values from 0 to 1023
- wavelet: float32 [8, 16], P(None, ('runs', 'shot')), parts along dimension 1, may hold values from -12 to 12
- receiver_cell: int32 [16, 256], P(('runs', 'shot')), parts along dimension 0, may hold values from 0 to 1023
- traces: float32 [8, 16, 256], P(None, ('runs', 'shot')), parts along dimension 1, may hold values from -10 to 10
- offset_perm: int32 [16], P('runs'), parts along dimension 0, may hold values from 0 to 7, each once
Outputs:
- offset_image: float32 [16, 64, 16, 256], P(('runs', 'shot'), 'slab'), parts along dimension 0
- source_final: float32 [16, 64, 16, 256], P(('runs', 'shot'), 'slab'), parts along dimension 0
- receiver_final: float32 [16, 64, 16, 256], P(('runs', 'shot'), 'slab'), parts along dimension 0
The draws below stay inside these ranges and needn't reach their ends.
There are 2 independent parts, one for each index of `runs`. The reference program is written for one: setup_inputs(seed, part) draws one part's arguments, and reference() takes and returns one part's arrays. A program takes and returns all parts, laid end to end along the dimension named above; each array names one. Nothing has to cross between parts.
Inputs may be any that keep to these rules, and one draw needn't show every extreme that they name: `source_cell`: a surface cell index. `receiver_cell`: surface cell indices; two receivers may share a cell. `offset_perm`: every offset index appears once.
All inputs are finite; a program needn't handle non-finite values.
Results may differ from the reference program's by a relative error of at most 0.0003.
Values sent between devices are 32-bit elements; how exact they have to be, the bound alone decides.
No kernel may reach another device: no remote copies, remote signals or barrier semaphores. Data moves between devices by JAX's collectives and lax.ppermute only.
A program may use at most 64 MiB of HBM per device.

```python
import math
import jax
import jax.numpy as jnp
from jax import lax

NY = 16
NZ = 256
RECV = 256
STEPS = 8
INJECT_Z = 4
NX = 64
SHOTS = 8
OFFSETS = 8


def with_ends(values, own_key, smallest, high):
    place = [jax.random.randint(jax.random.fold_in(own_key, axis), (), 0, length) for axis, length in enumerate(values.shape)]
    widest = values.shape.index(max(values.shape))
    next_to = place[:widest] + [(place[widest] + 1) % values.shape[widest]] + place[widest + 1:]
    return values.at[tuple(place)].set(smallest).at[tuple(next_to)].set(high)


def block_scale(stream_key, dims, split, least, largest):
    level, own = 1.0, jax.random.fold_in(stream_key, 6)
    for position, shards_of in split:
        steps = jnp.exp(jax.random.uniform(jax.random.fold_in(own, position), (shards_of,), jnp.float32, least / len(split), largest / len(split)))
        level = level * jnp.repeat(steps, dims[position] // shards_of).reshape([-1 if axis == position else 1 for axis in range(len(dims))])
    return level


def noise(own_key, extent, scale, reach, cuts=(), kind=jnp.bfloat16):
    entries = scale * jax.random.normal(own_key, extent, jnp.float32)
    if cuts:
        entries = entries * block_scale(own_key, extent, cuts, -0.22, 0.18)
    return jnp.clip(entries, -reach, reach).astype(kind)


def setup_inputs(seed: int = 0, part: int = 0) -> dict:
    keys = jax.random.split(jax.random.key(seed), 11)
    part_keys = jax.random.split(jax.random.fold_in(keys[10], part), 11)
    source_now = noise(part_keys[0], (SHOTS, NX, NY, NZ), 0.5, 4.0, ((0, 4), (1, 4)), jnp.float32)
    source_prev = noise(part_keys[1], (SHOTS, NX, NY, NZ), 0.5, 4.0, ((0, 4), (1, 4)), jnp.float32)
    receiver_now = noise(part_keys[2], (SHOTS, NX, NY, NZ), 0.5, 4.0, ((0, 4), (1, 4)), jnp.float32)
    receiver_prev = noise(part_keys[3], (SHOTS, NX, NY, NZ), 0.5, 4.0, ((0, 4), (1, 4)), jnp.float32)
    courant_sq = jnp.clip(jnp.exp(math.log(0.52) - 0.6931472 * jax.random.uniform(part_keys[4], (NX, NY, NZ), jnp.float32) ** block_scale(part_keys[4], (NX, NY, NZ), ((0, 4),), -0.2, 0.2)), 0.26, 0.52)
    source_cell = with_ends(jax.random.randint(part_keys[5], (SHOTS,), 0, NX * NY), jax.random.fold_in(part_keys[5], 1), 0, (NX * NY) - 1).astype(jnp.int32)
    wavelet = noise(part_keys[6], (STEPS, SHOTS), 3.0, 12.0, ((1, 4),), jnp.float32)
    receiver_cell = with_ends(jax.random.randint(part_keys[7], (SHOTS, RECV), 0, NX * NY), jax.random.fold_in(part_keys[7], 1), 0, (NX * NY) - 1).astype(jnp.int32)
    traces = noise(part_keys[8], (STEPS, SHOTS, RECV), 2.0, 10.0, ((1, 4),), jnp.float32)
    offset_perm = jax.random.permutation(part_keys[9], OFFSETS).astype(jnp.int32)
    return {"source_now": source_now, "source_prev": source_prev, "receiver_now": receiver_now, "receiver_prev": receiver_prev, "courant_sq": courant_sq, "source_cell": source_cell, "wavelet": wavelet, "receiver_cell": receiver_cell, "traces": traces, "offset_perm": offset_perm}


stencil_weights = (-205.0 / 72.0, 8.0 / 5.0, -1.0 / 5.0, 8.0 / 315.0, -1.0 / 560.0)
side_weight = 1.0 / 16.0


def laplace(wavefield):
    size_x, size_y, size_z = wavefield.shape[-3:]
    leading = [(0, 0)] * (wavefield.ndim - 3)
    padded = jnp.pad(wavefield, leading + [(4, 4)] * 3)
    summed = (1.0 + 2.0 * side_weight) * stencil_weights[0] * wavefield
    for distance in range(1, 5):
        weight = stencil_weights[distance]
        summed = summed + weight * (padded[..., 4 + distance:4 + distance + size_x, 4:4 + size_y, 4:4 + size_z] + padded[..., 4 - distance:4 - distance + size_x, 4:4 + size_y, 4:4 + size_z])
        summed = summed + side_weight * weight * (padded[..., 4:4 + size_x, 4 + distance:4 + distance + size_y, 4:4 + size_z] + padded[..., 4:4 + size_x, 4 - distance:4 - distance + size_y, 4:4 + size_z])
        summed = summed + side_weight * weight * (padded[..., 4:4 + size_x, 4:4 + size_y, 4 + distance:4 + distance + size_z] + padded[..., 4:4 + size_x, 4:4 + size_y, 4 - distance:4 - distance + size_z])
    return summed


def reference(source_now, source_prev, receiver_now, receiver_prev, courant_sq, source_cell, wavelet, receiver_cell, traces, offset_perm):
    fields = jnp.stack([source_now, receiver_now])
    before = jnp.stack([source_prev, receiver_prev])
    shot_index = jnp.arange(SHOTS, dtype=jnp.int32)
    shot_grid = jnp.broadcast_to(shot_index[:, None], receiver_cell.shape)
    for moment in range(STEPS):
        source_plane = jnp.zeros((SHOTS, NX * NY), jnp.float32).at[shot_index, source_cell].add(wavelet[moment])
        receiver_plane = jnp.zeros((SHOTS, NX * NY), jnp.float32).at[shot_grid, receiver_cell].add(traces[moment])
        planes = jnp.stack([source_plane, receiver_plane]).reshape(2, SHOTS, NX, NY)
        updated = 2.0 * fields - before + courant_sq * laplace(fields)
        updated = updated.at[:, :, :, :, INJECT_Z].add(planes)
        before, fields = fields, updated
    half_span = OFFSETS // 2
    source_pad = jnp.pad(fields[0], ((0, 0), (0, 0), (half_span, half_span), (0, 0)))
    receiver_pad = jnp.pad(fields[1], ((0, 0), (0, 0), (half_span, half_span), (0, 0)))

    def one_offset(lag_index):
        shift_by = lag_index - half_span
        shifted_source = lax.dynamic_slice_in_dim(source_pad, half_span - shift_by, NY, axis=2)
        shifted_receiver = lax.dynamic_slice_in_dim(receiver_pad, half_span + shift_by, NY, axis=2)
        return jnp.sum(shifted_source * shifted_receiver, axis=0)

    offset_image = lax.map(one_offset, offset_perm)
    return offset_image, fields[0], fields[1]
```

```python
import functools

import jax
import jax.numpy as jnp
from jax import lax
from jax.experimental import pallas as pl
from jax.experimental.pallas import tpu as pltpu
from jax.sharding import PartitionSpec as P

REACH = 4
INJECT_Z = 4
LANES = 128
CHUNK = 8

SCALE = 8.0 / 5.0
SIDE = 1.0 / 16.0
OWN = (1.0 + 2.0 * SIDE) * (-205.0 / 72.0) / SCALE
TAPS = (1.0, -1.0 / 8.0, 1.0 / 63.0, -1.0 / 896.0)

VMEM_LIMIT = 24 * 1024 * 1024


def vmem():
    return pl.BlockSpec(memory_space=pltpu.VMEM)


def smem():
    return pl.BlockSpec(memory_space=pltpu.SMEM)


def hbm():
    return pl.BlockSpec(memory_space=pl.ANY)


def params():
    return pltpu.CompilerParams(vmem_limit_bytes=VMEM_LIMIT)


def struct(shape, dtype=jnp.float32):
    return jax.ShapeDtypeStruct(shape, dtype)


def even_pairs(count):
    pairs = []
    for i in range(0, count - 1, 2):
        pairs += [(i, i + 1), (i + 1, i)]
    return pairs


def odd_pairs(count):
    pairs = []
    for i in range(1, count - 1, 2):
        pairs += [(i, i + 1), (i + 1, i)]
    return pairs


def trade(even_edge, odd_edge):
    count = lax.axis_size("slab")
    return (
        lax.ppermute(even_edge, "slab", even_pairs(count)),
        lax.ppermute(odd_edge, "slab", odd_pairs(count)),
    )


def parity():
    return lax.rem(lax.axis_index("slab"), 2)


def edge_starts(rows, width):
    odd = parity()
    return (1 - odd) * (rows - width), odd * (rows - width)


def halo_starts(rows, width):
    odd = parity()
    return (1 - odd) * (rows + width), odd * (rows + width)


def pack_kernel(groups, rows, *refs):
    source, receiver, courant = refs[:3]
    outs = refs[3 : 3 + 2 * groups]
    sem = refs[-1]
    copies = []
    for side, start in enumerate(edge_starts(rows, REACH)):
        planes = pl.ds(start, REACH)
        for group in range(groups):
            out = outs[2 * group + side]
            pieces = [source.at[group, planes], receiver.at[group, planes]]
            if group == 0:
                pieces.append(courant.at[planes])
            for index, piece in enumerate(pieces):
                copies.append(pltpu.make_async_copy(piece, out.at[index], sem.at[len(copies)]))
    for copy in copies:
        copy.start()
    for copy in copies:
        copy.wait()


def pack(source_now, receiver_now, courant_sq):
    groups, rows, size_y, size_z = source_now.shape
    shapes = []
    for group in range(groups):
        shapes += [struct((3 if group == 0 else 2, REACH, size_y, size_z))] * 2
    return pl.pallas_call(
        functools.partial(pack_kernel, groups, rows),
        out_shape=shapes,
        in_specs=[hbm()] * 3,
        out_specs=[vmem()] * len(shapes),
        scratch_shapes=[pltpu.SemaphoreType.DMA((2 * (2 * groups + 1),))],
        compiler_params=params(),
        name="pack",
    )(source_now, receiver_now, courant_sq)


def band(distance):
    value = jnp.zeros(distance.shape, jnp.float32)
    for step, tap in enumerate(TAPS):
        value = jnp.where(distance == step + 1, SIDE * tap, value)
    return value


def prepare_kernel(rows, source_cell, wavelet, receiver_cell, traces, along_z, along_y, *planes):
    groups = len(planes)
    _, plane_count, size_y, _ = planes[0].shape
    steps = traces.shape[0]
    size_z = along_z.shape[0]
    block = along_y.shape[0]
    row = lax.broadcasted_iota(jnp.int32, (size_z, size_z), 0)
    col = lax.broadcasted_iota(jnp.int32, (size_z, size_z), 1)
    along_z[...] = band(jnp.abs(row - col)).astype(jnp.bfloat16)
    row = lax.broadcasted_iota(jnp.int32, (block, block), 0)
    col = lax.broadcasted_iota(jnp.int32, (block, block), 1)
    same = lax.div(row, size_y) == lax.div(col, size_y)
    half = jnp.where(same, band(jnp.abs(row - col)), 0.0).astype(jnp.bfloat16)
    along_y[:, :block] = half
    along_y[:, block:] = half
    first = (lax.axis_index("slab") * rows - REACH) * size_y
    cells = plane_count * size_y
    lane = lax.broadcasted_iota(jnp.int32, (1, LANES), 1)
    for group in range(groups):
        ids = first + lax.broadcasted_iota(jnp.int32, (cells, 1), 0)
        amplitude = jnp.zeros((1, LANES), jnp.float32)
        for step in range(steps):
            amplitude = jnp.where(lane == step, wavelet[step, group], amplitude)
        hit = jnp.broadcast_to(ids, (cells, LANES)) == source_cell[group]
        spread = jnp.where(hit, jnp.broadcast_to(amplitude, (cells, LANES)), 0.0)
        planes[group][0] = spread.reshape(plane_count, size_y, LANES)
        count = receiver_cell.shape[1]
        wide = first + lax.broadcasted_iota(jnp.int32, (cells, count), 0)
        here = jnp.broadcast_to(receiver_cell[group : group + 1, :], (cells, count))
        hot = (wide == here).astype(jnp.float32)
        data = traces[:, group, :]
        data = jnp.concatenate([data, jnp.zeros((LANES - steps, count), jnp.float32)], axis=0)
        summed = lax.dot_general(
            hot,
            data,
            (((1,), (1,)), ((), ())),
            precision=lax.Precision.HIGHEST,
            preferred_element_type=jnp.float32,
        )
        planes[group][1] = summed.reshape(plane_count, size_y, LANES)


def prepare(source_cell, wavelet, receiver_cell, traces, rows, size_y, size_z):
    groups = source_cell.shape[0]
    block = CHUNK * size_y
    return pl.pallas_call(
        functools.partial(prepare_kernel, rows),
        out_shape=[
            struct((size_z, size_z), jnp.bfloat16),
            struct((block, 2 * block), jnp.bfloat16),
        ]
        + [struct((2, rows + 2 * REACH, size_y, LANES))] * groups,
        in_specs=[smem(), smem(), vmem(), vmem()],
        out_specs=[vmem()] * (2 + groups),
        compiler_params=params(),
        name="prepare",
    )(source_cell, wavelet, receiver_cell, traces)


def advance(now, first, before, before_first, courant, courant_first, inject, inject_first, step, along_z, along_y, write):
    size_y, size_z = now.shape[-2:]
    value = now[first : first + CHUNK].reshape(CHUNK * size_y, size_z)
    high = value.astype(jnp.bfloat16)
    low = (value - high.astype(jnp.float32)).astype(jnp.bfloat16)
    dot = functools.partial(jnp.dot, preferred_element_type=jnp.float32)
    sides = dot(high, along_z) + dot(low, along_z)
    sides = sides + dot(along_y, jnp.concatenate([high, low], axis=0))
    lane = lax.broadcasted_iota(jnp.int32, (size_y, LANES), 1)
    for i in range(CHUNK):
        at = first + i
        own = now[at]
        total = sides[i * size_y : (i + 1) * size_y] + OWN * own
        for distance, tap in enumerate(TAPS, 1):
            pair = now[at + distance] + now[at - distance]
            total = total + (pair if tap == 1.0 else tap * pair)
        new = (own + own) - before[before_first + i] + courant[courant_first + i] * total
        spot = pltpu.roll(inject[inject_first + i], (INJECT_Z - step) % LANES, 1)
        near = new[:, :LANES] + jnp.where(lane == INJECT_Z, spot, 0.0)
        write(i, jnp.concatenate([near, new[:, LANES:]], axis=1))


def first_kernel(group, rows, has_courant, width, source, receiver, source_before, receiver_before, courant, even, odd, inject, along_z, along_y, *refs):
    fresh, held, even_edge, odd_edge = refs[:4]
    before, sem = refs[-2:]
    copies = []
    for kind, (own, past) in enumerate(((source, source_before), (receiver, receiver_before))):
        copies.append(pltpu.make_async_copy(own.at[group], held.at[kind, pl.ds(REACH, rows)], sem.at[2 * kind]))
        copies.append(pltpu.make_async_copy(past.at[group], before.at[kind], sem.at[2 * kind + 1]))
    for copy in copies:
        copy.start()
    even_at, odd_at = halo_starts(rows, REACH)
    if has_courant:
        scaled = refs[4]
        scaled[REACH : REACH + rows] = SCALE * courant[...]
        scaled[pl.ds(even_at, REACH)] = SCALE * even[2]
        scaled[pl.ds(odd_at, REACH)] = SCALE * odd[2]
    else:
        scaled = courant
    z_band, y_band = along_z[...], along_y[...]
    for kind in range(2):
        field = held.at[kind]
        field[pl.ds(even_at, REACH)] = even[kind]
        field[pl.ds(odd_at, REACH)] = odd[kind]
        copies[2 * kind].wait()
        copies[2 * kind + 1].wait()
        for at in range(0, rows, CHUNK):

            def write(i, new, kind=kind, at=at):
                fresh[kind, at + i] = new

            advance(field, REACH + at, before.at[kind], at, scaled, REACH + at, inject.at[kind], REACH + at, 0, z_band, y_band, write)
    send(rows, width, fresh, even_edge, odd_edge)


def send(rows, width, fresh, even_edge, odd_edge):
    even_from, odd_from = edge_starts(rows, width)
    even_edge[...] = fresh[:, pl.ds(even_from, width)]
    odd_edge[...] = fresh[:, pl.ds(odd_from, width)]


def first_round(group, width, fields, courant, halos, inject, along_z, along_y):
    rows, size_y, size_z = fields[0].shape[1:]
    has_courant = group == 0
    edge = struct((2, width, size_y, size_z))
    shapes = [struct((2, rows, size_y, size_z)), struct((2, rows + 2 * REACH, size_y, size_z)), edge, edge]
    if has_courant:
        shapes.append(struct((rows + 2 * REACH, size_y, size_z)))
    return pl.pallas_call(
        functools.partial(first_kernel, group, rows, has_courant, width),
        out_shape=shapes,
        in_specs=[hbm()] * 4 + [vmem()] * 6,
        out_specs=[vmem()] * len(shapes),
        scratch_shapes=[pltpu.VMEM((2, rows, size_y, size_z), jnp.float32), pltpu.SemaphoreType.DMA((4,))],
        compiler_params=params(),
        name=f"first_{group}",
    )(*fields, courant, *halos, inject, along_z, along_y)


def pair_kernel(rows, step, width, now, before, even, odd, courant, inject, along_z, along_y, fresh, held, even_edge, odd_edge, wide):
    reach = 2 * REACH
    even_at, odd_at = halo_starts(rows, reach)
    z_band, y_band = along_z[...], along_y[...]
    for kind in range(2):
        field = wide.at[kind]
        field[reach : reach + rows] = now[kind]
        field[pl.ds(even_at, reach)] = even[kind]
        field[pl.ds(odd_at, reach)] = odd[kind]
        middle = held.at[kind]
        for at in range(0, rows + 2 * REACH, CHUNK):

            def write_middle(i, new, kind=kind, at=at):
                held[kind, at + i] = new

            advance(field, REACH + at, before.at[kind], at, courant, at, inject.at[kind], at, step, z_band, y_band, write_middle)
        for at in range(0, rows, CHUNK):

            def write(i, new, kind=kind, at=at):
                fresh[kind, at + i] = new

            advance(middle, REACH + at, field, reach + at, courant, REACH + at, inject.at[kind], REACH + at, step + 1, z_band, y_band, write)
    send(rows, width, fresh, even_edge, odd_edge)


def pair_round(group, step, width, now, before, halos, courant, inject, along_z, along_y):
    rows, size_y, size_z = now.shape[1:]
    edge = struct((2, width, size_y, size_z))
    shapes = [struct(now.shape), struct((2, rows + 2 * REACH, size_y, size_z)), edge, edge]
    return pl.pallas_call(
        functools.partial(pair_kernel, rows, step, width),
        out_shape=shapes,
        in_specs=[vmem()] * 8,
        out_specs=[vmem()] * 4,
        scratch_shapes=[pltpu.VMEM((2, rows + 4 * REACH, size_y, size_z), jnp.float32)],
        compiler_params=params(),
        name=f"pair_{group}_{step}",
    )(now, before, *halos, courant, inject, along_z, along_y)


def last_kernel(group, rows, step, now, before, even, odd, courant, inject, along_z, along_y, *refs):
    final, source_out, receiver_out, wide, sem = refs[-5:]
    even_at, odd_at = halo_starts(rows, REACH)
    z_band, y_band = along_z[...], along_y[...]
    copies = []
    for kind, out in enumerate((source_out, receiver_out)):
        field = wide.at[kind]
        field[REACH : REACH + rows] = now[kind]
        field[pl.ds(even_at, REACH)] = even[kind]
        field[pl.ds(odd_at, REACH)] = odd[kind]
        for at in range(0, rows, CHUNK):

            def write(i, new, kind=kind, at=at):
                final[kind, at + i] = new

            advance(field, REACH + at, before.at[kind], REACH + at, courant, REACH + at, inject.at[kind], REACH + at, step, z_band, y_band, write)
        copies.append(pltpu.make_async_copy(final.at[kind], out.at[group], sem.at[kind]))
        copies[kind].start()
    for copy in copies:
        copy.wait()


def last_round(group, groups, step, now, before, halos, courant, inject, along_z, along_y, outs):
    rows, size_y, size_z = now.shape[1:]
    whole = struct((groups, rows, size_y, size_z))
    return pl.pallas_call(
        functools.partial(last_kernel, group, rows, step),
        out_shape=[struct(now.shape), whole, whole],
        in_specs=[vmem()] * 8 + [hbm()] * len(outs),
        out_specs=[vmem(), hbm(), hbm()],
        scratch_shapes=[pltpu.VMEM((2, rows + 2 * REACH, size_y, size_z), jnp.float32), pltpu.SemaphoreType.DMA((2,))],
        input_output_aliases={8: 1, 9: 2} if outs else {},
        compiler_params=params(),
        name=f"last_{group}",
    )(now, before, *halos, courant, inject, along_z, along_y, *outs)


def shifted(plane, amount):
    size_y = plane.shape[0]
    if amount == 0:
        return plane
    if abs(amount) >= size_y:
        return jnp.zeros_like(plane)
    row = lax.broadcasted_iota(jnp.int32, plane.shape, 0)
    inside = (row >= amount) if amount > 0 else (row < size_y + amount)
    return jnp.where(inside, pltpu.roll(plane, amount % size_y, 0), 0.0)


def image_kernel(ahead, slots, offset_perm, *refs):
    fields, image = refs[:-1], refs[-1]
    count = offset_perm.shape[0]
    half_span = count // 2
    rows = image.shape[1]
    here = lax.axis_index("shot")
    pairs = lax.axis_size("shot") // 2
    owner = 2 * lax.rem(lax.div(here, 2) + ahead, pairs) + lax.rem(here, 2)

    def one_slot(slot, carry):
        index = offset_perm[owner * slots + slot]
        for lag_index in range(count):
            lag = lag_index - half_span

            @pl.when(index == lag_index)
            def _(lag=lag):
                def one_plane(x, carry):
                    total = None
                    for field in fields:
                        term = field[1, x] * shifted(field[0, x], 2 * lag)
                        total = term if total is None else total + term
                    image[slot, x] = shifted(total, -lag)
                    return carry

                lax.fori_loop(0, rows, one_plane, 0, unroll=2)

        return carry

    lax.fori_loop(0, slots, one_slot, 0)


def image_part(ahead, slots, offset_perm, fields):
    _, rows, size_y, size_z = fields[0].shape
    return pl.pallas_call(
        functools.partial(image_kernel, ahead, slots),
        out_shape=struct((slots, rows, size_y, size_z)),
        in_specs=[smem()] + [vmem()] * len(fields),
        out_specs=vmem(),
        compiler_params=params(),
        name=f"image_{ahead}",
    )(offset_perm, *fields)


def body(source_now, source_prev, receiver_now, receiver_prev, courant_sq, source_cell, wavelet, receiver_cell, traces, offset_perm):
    groups, rows, size_y, size_z = source_now.shape
    steps = wavelet.shape[0]
    shot_devices = lax.axis_size("shot")
    slots = offset_perm.shape[0] // shot_devices
    everyone = range(groups)

    edges = pack(source_now, receiver_now, courant_sq)
    halos = [trade(edges[2 * g], edges[2 * g + 1]) for g in everyone]
    along_z, along_y, *inject = prepare(source_cell, wavelet, receiver_cell, traces, rows, size_y, size_z)

    fields = (source_now, receiver_now, source_prev, receiver_prev)
    now, before = [None] * groups, [None] * groups
    courant = courant_sq
    for g in everyone:
        result = first_round(g, 2 * REACH, fields, courant, halos[g], inject[g], along_z, along_y)
        now[g], before[g] = result[:2]
        if g == 0:
            courant = result[4]
        halos[g] = trade(*result[2:4])
    for step in range(1, steps - 1, 2):
        width = 2 * REACH if step + 2 < steps - 1 else REACH
        for g in everyone:
            now[g], before[g], even, odd = pair_round(g, step, width, now[g], before[g], halos[g], courant, inject[g], along_z, along_y)
            halos[g] = trade(even, odd)
    outs = ()
    final, other = [None] * groups, [None] * groups
    swap = [(i, i ^ 1) for i in range(shot_devices)]
    for g in everyone:
        final[g], *outs = last_round(g, groups, steps - 1, now[g], before[g], halos[g], courant, inject[g], along_z, along_y, outs)
        other[g] = lax.ppermute(final[g], "shot", swap)

    pairs = shot_devices // 2
    arrived = []
    for ahead in range(1, pairs):
        part = image_part(ahead, slots, offset_perm, final + other)
        route = [(2 * p + c, 2 * ((p + ahead) % pairs) + c) for p in range(pairs) for c in range(2)]
        arrived.append(lax.ppermute(part, "shot", route))
    image = image_part(0, slots, offset_perm, final + other)
    for part in arrived:
        image = image + part
    return (image, *outs)


def solution(mesh):
    shots = ("runs", "shot")
    in_specs = (
        P(shots, "slab", None, None),
        P(shots, "slab", None, None),
        P(shots, "slab", None, None),
        P(shots, "slab", None, None),
        P(("runs", "slab"), None, None),
        P(shots),
        P(None, shots),
        P(shots, None),
        P(None, shots, None),
        P("runs"),
    )
    out_specs = (P(shots, "slab", None, None),) * 3
    return jax.shard_map(body, mesh=mesh, in_specs=in_specs, out_specs=out_specs, check_vma=False)
```

```python
import functools

import jax
import jax.numpy as jnp
from jax import lax
from jax.experimental import pallas as pl
from jax.experimental.pallas import tpu as pltpu
from jax.sharding import PartitionSpec as P


REACH = 4
INJECT_Z = 4
LANES = 128
CHUNK = 8

SCALE = 8.0 / 5.0
SIDE = 1.0 / 16.0
OWN = (1.0 + 2.0 * SIDE) * (-205.0 / 72.0) / SCALE
TAPS = (1.0, -1.0 / 8.0, 1.0 / 63.0, -1.0 / 896.0)

VMEM_LIMIT = 24 * 1024 * 1024


def vmem():
    return pl.BlockSpec(memory_space=pltpu.VMEM)


def smem():
    return pl.BlockSpec(memory_space=pltpu.SMEM)


def hbm():
    return pl.BlockSpec(memory_space=pltpu.HBM)


def params():
    return pltpu.CompilerParams(vmem_limit_bytes=VMEM_LIMIT)


def struct(shape, dtype=jnp.float32):
    return jax.ShapeDtypeStruct(shape, dtype)


def even_pairs(count):
    pairs = []
    for i in range(0, count - 1, 2):
        pairs += [(i, i + 1), (i + 1, i)]
    return pairs


def odd_pairs(count):
    pairs = []
    for i in range(1, count - 1, 2):
        pairs += [(i, i + 1), (i + 1, i)]
    return pairs


def trade(even_edge, odd_edge):
    count = lax.axis_size("slab")
    even = lax.ppermute(even_edge, "slab", even_pairs(count))
    odd = lax.ppermute(odd_edge, "slab", odd_pairs(count))
    return even, odd


def parity():
    return lax.rem(lax.axis_index("slab"), 2)


def edge_starts(rows, width):
    odd = parity()
    return (1 - odd) * (rows - width), odd * (rows - width)


def halo_starts(rows, width):
    odd = parity()
    return (1 - odd) * (rows + width), odd * (rows + width)


def pack_kernel(groups, rows, *refs):
    source, receiver, courant = refs[:3]
    outs = refs[3 : 3 + 2 * groups]
    sem = refs[-1]
    copies = []
    for side, start in enumerate(edge_starts(rows, REACH)):
        planes = pl.ds(start, REACH)
        for group in range(groups):
            out = outs[2 * group + side]
            pieces = [source.at[group, planes], receiver.at[group, planes]]
            if group == 0:
                pieces.append(courant.at[planes])
            for index, piece in enumerate(pieces):
                copies.append(pltpu.make_async_copy(piece, out.at[index], sem.at[len(copies)]))
    for copy in copies:
        copy.start()
    for copy in copies:
        copy.wait()


def stay(*arrays):
    return [pltpu.with_memory_space_constraint(array, pltpu.HBM) for array in arrays]


def pack(source_now, receiver_now, courant_sq):
    groups, rows, size_y, size_z = source_now.shape
    shapes = []
    for group in range(groups):
        shapes += [struct((3 if group == 0 else 2, REACH, size_y, size_z))] * 2
    return pl.pallas_call(
        functools.partial(pack_kernel, groups, rows),
        out_shape=shapes,
        in_specs=[hbm()] * 3,
        out_specs=[vmem()] * len(shapes),
        scratch_shapes=[pltpu.SemaphoreType.DMA((2 * (2 * groups + 1),))],
        compiler_params=params(),
        name="pack",
    )(*stay(source_now, receiver_now, courant_sq))


def band(distance):
    value = jnp.zeros(distance.shape, jnp.float32)
    for step, tap in enumerate(TAPS):
        value = jnp.where(distance == step + 1, SIDE * tap, value)
    return value


def prepare_kernel(groups, rows, source_cell, wavelet, receiver_cell, traces, source, receiver, source_before, receiver_before, along_z, along_y, *refs):
    planes, now, before, sem = refs[:groups], refs[groups : 2 * groups], refs[2 * groups : 3 * groups], refs[-1]
    copies = []
    for group in range(groups):
        pieces = ((source, now, 0), (receiver, now, 1), (source_before, before, 0), (receiver_before, before, 1))
        for array, place, kind in pieces:
            copies.append(pltpu.make_async_copy(array.at[group], place[group].at[kind], sem.at[len(copies)]))
    for copy in copies:
        copy.start()
    _, plane_count, size_y, _ = planes[0].shape
    steps = traces.shape[0]
    size_z = along_z.shape[0]
    block = along_y.shape[0]
    row = lax.broadcasted_iota(jnp.int32, (size_z, size_z), 0)
    col = lax.broadcasted_iota(jnp.int32, (size_z, size_z), 1)
    along_z[...] = band(jnp.abs(row - col)).astype(jnp.bfloat16)
    row = lax.broadcasted_iota(jnp.int32, (block, block), 0)
    col = lax.broadcasted_iota(jnp.int32, (block, block), 1)
    same = lax.div(row, size_y) == lax.div(col, size_y)
    half = jnp.where(same, band(jnp.abs(row - col)), 0.0).astype(jnp.bfloat16)
    along_y[:, :block] = half
    along_y[:, block:] = half
    first = (lax.axis_index("slab") * rows - REACH) * size_y
    cells = plane_count * size_y
    lane = lax.broadcasted_iota(jnp.int32, (1, LANES), 1)
    for group in range(groups):
        ids = first + lax.broadcasted_iota(jnp.int32, (cells, 1), 0)
        amplitude = jnp.zeros((1, LANES), jnp.float32)
        for step in range(steps):
            amplitude = jnp.where(lane == step, wavelet[step, group], amplitude)
        hit = jnp.broadcast_to(ids, (cells, LANES)) == source_cell[group]
        spread = jnp.where(hit, jnp.broadcast_to(amplitude, (cells, LANES)), 0.0)
        planes[group][0] = spread.reshape(plane_count, size_y, LANES)
        count = receiver_cell.shape[1]
        wide = first + lax.broadcasted_iota(jnp.int32, (cells, count), 0)
        here = jnp.broadcast_to(receiver_cell[group : group + 1, :], (cells, count))
        hot = (wide == here).astype(jnp.float32)
        data = traces[:, group, :]
        data = jnp.concatenate([data, jnp.zeros((LANES - steps, count), jnp.float32)], axis=0)
        summed = lax.dot_general(
            hot,
            data,
            (((1,), (1,)), ((), ())),
            precision=lax.Precision.HIGHEST,
            preferred_element_type=jnp.float32,
        )
        planes[group][1] = summed.reshape(plane_count, size_y, LANES)
    for copy in copies:
        copy.wait()


def prepare(source_cell, wavelet, receiver_cell, traces, fields):
    groups, rows, size_y, size_z = fields[0].shape
    block = CHUNK * size_y
    return pl.pallas_call(
        functools.partial(prepare_kernel, groups, rows),
        out_shape=[
            struct((size_z, size_z), jnp.bfloat16),
            struct((block, 2 * block), jnp.bfloat16),
        ]
        + [struct((2, rows + 2 * REACH, size_y, LANES))] * groups
        + [struct((2, rows, size_y, size_z))] * (2 * groups),
        in_specs=[smem(), smem(), vmem(), vmem()] + [hbm()] * 4,
        out_specs=[vmem()] * (2 + 3 * groups),
        scratch_shapes=[pltpu.SemaphoreType.DMA((4 * groups,))],
        compiler_params=params(),
        name="prepare",
    )(source_cell, wavelet, receiver_cell, traces, *stay(*fields))


def advance(now, at, before, before_at, courant, courant_at, inject, inject_at, runs, step, along_z, along_y, write):
    size_y, size_z = now.shape[-2:]
    pieces = [now[at + first : at + first + count].reshape(count * size_y, size_z) for first, count in runs]
    value = pieces[0] if len(pieces) == 1 else jnp.concatenate(pieces, axis=0)
    high = value.astype(jnp.bfloat16)
    low = (value - high.astype(jnp.float32)).astype(jnp.bfloat16)
    dot = functools.partial(jnp.dot, preferred_element_type=jnp.float32)
    sides = dot(high, along_z) + dot(low, along_z)
    sides = sides + dot(along_y, jnp.concatenate([high, low], axis=0))
    lane = lax.broadcasted_iota(jnp.int32, (size_y, LANES), 1)
    for i, plane in enumerate(first + j for first, count in runs for j in range(count)):
        here = at + plane
        own = now[here]
        total = sides[i * size_y : (i + 1) * size_y] + OWN * own
        for distance, tap in enumerate(TAPS, 1):
            pair = now[here + distance] + now[here - distance]
            total = total + (pair if tap == 1.0 else tap * pair)
        new = (own + own) - before[before_at + plane] + courant[courant_at + plane] * total
        spot = pltpu.roll(inject[inject_at + plane], (INJECT_Z - step) % LANES, 1)
        near = new[:, :LANES] + jnp.where(lane == INJECT_Z, spot, 0.0)
        write(i, plane, jnp.concatenate([near, new[:, LANES:]], axis=1))


def chunks(start, stop):
    return [[(at, CHUNK)] for at in range(start, stop, CHUNK)]


def first_kernel(rows, has_courant, width, now, before, courant, even, odd, inject, along_z, along_y, fresh, held, even_edge, odd_edge, *scaled):
    even_at, odd_at = halo_starts(rows, REACH)
    if has_courant:
        (courant_out,) = scaled
        courant_out[REACH : REACH + rows] = SCALE * courant[...]
        courant_out[pl.ds(even_at, REACH)] = SCALE * even[2]
        courant_out[pl.ds(odd_at, REACH)] = SCALE * odd[2]
        courant = courant_out
    z_band, y_band = along_z[...], along_y[...]
    for kind in range(2):
        field = held.at[kind]
        field[REACH : REACH + rows] = now[kind]
        field[pl.ds(even_at, REACH)] = even[kind]
        field[pl.ds(odd_at, REACH)] = odd[kind]

        def write(i, plane, new, kind=kind):
            fresh[kind, plane] = new

        for runs in chunks(0, rows):
            advance(field, REACH, before.at[kind], 0, courant, REACH, inject.at[kind], REACH, runs, 0, z_band, y_band, write)
    send(rows, width, fresh, even_edge, odd_edge)


def send(rows, width, fresh, even_edge, odd_edge):
    even_from, odd_from = edge_starts(rows, width)
    even_edge[...] = fresh[:, pl.ds(even_from, width)]
    odd_edge[...] = fresh[:, pl.ds(odd_from, width)]


def first_round(group, width, now, before, courant, halos, inject, along_z, along_y):
    rows, size_y, size_z = now.shape[1:]
    has_courant = group == 0
    edge = struct((2, width, size_y, size_z))
    shapes = [struct(now.shape), struct((2, rows + 2 * REACH, size_y, size_z)), edge, edge]
    if has_courant:
        shapes.append(struct((rows + 2 * REACH, size_y, size_z)))
    return pl.pallas_call(
        functools.partial(first_kernel, rows, has_courant, width),
        out_shape=shapes,
        in_specs=[vmem()] * 8,
        out_specs=[vmem()] * len(shapes),
        compiler_params=params(),
    )(now, before, courant, *halos, inject, along_z, along_y)


def pair_kernel(rows, step, width, now, before, even, odd, courant, inject, along_z, along_y, fresh, held, even_edge, odd_edge, wide):
    reach = 2 * REACH
    even_at, odd_at = halo_starts(rows, reach)
    z_band, y_band = along_z[...], along_y[...]
    for kind in range(2):
        field = wide.at[kind]
        field[reach : reach + rows] = now[kind]
        field[pl.ds(even_at, reach)] = even[kind]
        field[pl.ds(odd_at, reach)] = odd[kind]
        middle = held.at[kind]

        def write_middle(i, plane, new, kind=kind):
            held[kind, REACH + plane] = new

        def write(i, plane, new, kind=kind):
            fresh[kind, plane] = new

        for runs in chunks(-REACH, rows + REACH):
            advance(field, reach, before.at[kind], REACH, courant, REACH, inject.at[kind], REACH, runs, step, z_band, y_band, write_middle)
        for runs in chunks(0, rows):
            advance(middle, REACH, field, reach, courant, REACH, inject.at[kind], REACH, runs, step + 1, z_band, y_band, write)
    send(rows, width, fresh, even_edge, odd_edge)


def pair_round(step, width, now, before, halos, courant, inject, along_z, along_y):
    rows, size_y, size_z = now.shape[1:]
    edge = struct((2, width, size_y, size_z))
    shapes = [struct(now.shape), struct((2, rows + 2 * REACH, size_y, size_z)), edge, edge]
    return pl.pallas_call(
        functools.partial(pair_kernel, rows, step, width),
        out_shape=shapes,
        in_specs=[vmem()] * 8,
        out_specs=[vmem()] * 4,
        scratch_shapes=[pltpu.VMEM((2, rows + 4 * REACH, size_y, size_z), jnp.float32)],
        compiler_params=params(),
    )(now, before, *halos, courant, inject, along_z, along_y)


def inner_kernel(group, rows, step, now, before, courant, inject, along_z, along_y, *refs):
    final, source_out, receiver_out, sem = refs[-4:]
    count = rows - 2 * REACH
    z_band, y_band = along_z[...], along_y[...]
    copies = []
    for kind, out in enumerate((source_out, receiver_out)):

        def write(i, plane, new, kind=kind):
            final[kind, plane - REACH] = new

        for runs in chunks(REACH, rows - REACH):
            advance(now.at[kind], 0, before.at[kind], REACH, courant, REACH, inject.at[kind], REACH, runs, step, z_band, y_band, write)
        copies.append(pltpu.make_async_copy(final.at[kind], out.at[group, pl.ds(REACH, count)], sem.at[kind]))
        copies[kind].start()
    for copy in copies:
        copy.wait()


def inner_round(group, groups, step, now, before, courant, inject, along_z, along_y, outs):
    rows, size_y, size_z = now.shape[1:]
    whole = struct((groups, rows, size_y, size_z))
    return pl.pallas_call(
        functools.partial(inner_kernel, group, rows, step),
        out_shape=[struct((2, rows - 2 * REACH, size_y, size_z)), whole, whole],
        in_specs=[vmem()] * 6 + [hbm()] * len(outs),
        out_specs=[vmem(), hbm(), hbm()],
        scratch_shapes=[pltpu.SemaphoreType.DMA((2,))],
        input_output_aliases={6: 1, 7: 2} if outs else {},
        compiler_params=params(),
    )(now, before, courant, inject, along_z, along_y, *outs)


def outer_kernel(group, rows, step, now, before, even, odd, courant, inject, along_z, along_y, *refs):
    final, source_out, receiver_out, wide, sem = refs[-5:]
    even_at, odd_at = halo_starts(rows, REACH)
    z_band, y_band = along_z[...], along_y[...]
    copies = []
    for kind, out in enumerate((source_out, receiver_out)):
        field = wide.at[kind]
        field[REACH : REACH + rows] = now[kind]
        field[pl.ds(even_at, REACH)] = even[kind]
        field[pl.ds(odd_at, REACH)] = odd[kind]

        def write(i, plane, new, kind=kind):
            final[kind, i] = new

        runs = [(0, REACH), (rows - REACH, REACH)]
        advance(field, REACH, before.at[kind], REACH, courant, REACH, inject.at[kind], REACH, runs, step, z_band, y_band, write)
        for side, (first, count) in enumerate(runs):
            piece = final.at[kind, pl.ds(side * REACH, REACH)]
            copies.append(pltpu.make_async_copy(piece, out.at[group, pl.ds(first, count)], sem.at[2 * kind + side]))
            copies[-1].start()
    for copy in copies:
        copy.wait()


def outer_round(group, step, now, before, halos, courant, inject, along_z, along_y, outs):
    rows, size_y, size_z = now.shape[1:]
    return pl.pallas_call(
        functools.partial(outer_kernel, group, rows, step),
        out_shape=[struct((2, 2 * REACH, size_y, size_z))] + [struct(out.shape) for out in outs],
        in_specs=[vmem()] * 8 + [hbm()] * len(outs),
        out_specs=[vmem(), hbm(), hbm()],
        scratch_shapes=[pltpu.VMEM((2, rows + 2 * REACH, size_y, size_z), jnp.float32), pltpu.SemaphoreType.DMA((4,))],
        input_output_aliases={8: 1, 9: 2},
        compiler_params=params(),
    )(now, before, *halos, courant, inject, along_z, along_y, *outs)


def shifted(plane, amount):
    size_y = plane.shape[0]
    if amount == 0:
        return plane
    if abs(amount) >= size_y:
        return jnp.zeros_like(plane)
    row = lax.broadcasted_iota(jnp.int32, plane.shape, 0)
    inside = (row >= amount) if amount > 0 else (row < size_y + amount)
    return jnp.where(inside, pltpu.roll(plane, amount % size_y, 0), 0.0)


def partial_image(ahead, offset_perm, fields, image, others=()):
    count = offset_perm.shape[0]
    half_span = count // 2
    slots, rows = image.shape[:2]
    here = lax.axis_index("shot")
    pairs = lax.axis_size("shot") // 2
    owner = 2 * lax.rem(lax.div(here, 2) + ahead, pairs) + lax.rem(here, 2)

    def one_slot(slot, carry):
        index = offset_perm[owner * slots + slot]
        for lag_index in range(count):
            lag = lag_index - half_span

            @pl.when(index == lag_index)
            def _(lag=lag):
                def one_plane(x, carry):
                    total = None
                    for field in fields:
                        term = field[1, x] * shifted(field[0, x], 2 * lag)
                        total = term if total is None else total + term
                    total = shifted(total, -lag)
                    for other in others:
                        total = total + other[slot, x]
                    image[slot, x] = total
                    return carry

                lax.fori_loop(0, rows, one_plane, 0, unroll=2)

        return carry

    lax.fori_loop(0, slots, one_slot, 0)


def image_kernel(ahead, offset_perm, *refs):
    partial_image(ahead, offset_perm, refs[:-1], refs[-1])


def image_part(ahead, slots, offset_perm, fields):
    _, rows, size_y, size_z = fields[0].shape
    return pl.pallas_call(
        functools.partial(image_kernel, ahead),
        out_shape=struct((slots, rows, size_y, size_z)),
        in_specs=[smem()] + [vmem()] * len(fields),
        out_specs=vmem(),
        compiler_params=params(),
    )(offset_perm, *fields)


def inner_image_kernel(shots, offset_perm, *refs):
    inner_fields, outer_fields = refs[:shots], refs[shots : 2 * shots]
    others = refs[2 * shots : -4]
    image, outer, inner, sem = refs[-4:]
    partial_image(0, offset_perm, inner_fields, inner, others)
    copy = pltpu.make_async_copy(inner, image.at[:, pl.ds(REACH, inner.shape[1])], sem)
    copy.start()
    partial_image(0, offset_perm, outer_fields, outer)
    copy.wait()


def inner_image(slots, rows, offset_perm, inner_fields, outer_fields, others):
    _, inner_rows, size_y, size_z = inner_fields[0].shape
    shots = len(inner_fields)
    return pl.pallas_call(
        functools.partial(inner_image_kernel, shots),
        out_shape=[struct((slots, rows, size_y, size_z)), struct((slots, 2 * REACH, size_y, size_z))],
        in_specs=[smem()] + [vmem()] * (2 * shots + len(others)),
        out_specs=[hbm(), vmem()],
        scratch_shapes=[pltpu.VMEM((slots, inner_rows, size_y, size_z), jnp.float32), pltpu.SemaphoreType.DMA(())],
        compiler_params=params(),
        name="image_inner",
    )(offset_perm, *inner_fields, *outer_fields, *others)


def outer_image_kernel(rows, *refs):
    own, others = refs[0], refs[1:-4]
    image, outer, sem = refs[-3:]
    copies = []
    for side, first in enumerate((0, rows - REACH)):
        planes = pl.ds(side * REACH, REACH)
        total = own[:, planes]
        for other in others:
            total = total + other[:, planes]
        outer[:, planes] = total
        copies.append(pltpu.make_async_copy(outer.at[:, planes], image.at[:, pl.ds(first, REACH)], sem.at[side]))
        copies[side].start()
    for copy in copies:
        copy.wait()


def outer_image(image, own, others):
    return pl.pallas_call(
        functools.partial(outer_image_kernel, image.shape[1]),
        out_shape=struct(image.shape),
        in_specs=[vmem()] * (1 + len(others)) + [hbm()],
        out_specs=hbm(),
        scratch_shapes=[pltpu.VMEM(own.shape, jnp.float32), pltpu.SemaphoreType.DMA((2,))],
        input_output_aliases={1 + len(others): 0},
        compiler_params=params(),
        name="image_outer",
    )(own, *others, image)


def program(source_now, source_prev, receiver_now, receiver_prev, courant_sq, source_cell, wavelet, receiver_cell, traces, offset_perm):
    groups, rows, _, _ = source_now.shape
    steps = wavelet.shape[0]
    shot_devices = lax.axis_size("shot")
    slots = offset_perm.shape[0] // shot_devices
    everyone = range(groups)

    edges = pack(source_now, receiver_now, courant_sq)
    halos = [trade(edges[2 * g], edges[2 * g + 1]) for g in everyone]
    fields = (source_now, receiver_now, source_prev, receiver_prev)
    along_z, along_y, *rest = prepare(source_cell, wavelet, receiver_cell, traces, fields)
    inject, now, before = rest[:groups], rest[groups : 2 * groups], rest[2 * groups :]

    courant = courant_sq
    for g in everyone:
        result = first_round(g, 2 * REACH, now[g], before[g], courant, halos[g], inject[g], along_z, along_y)
        now[g], before[g] = result[:2]
        if g == 0:
            courant = result[4]
        halos[g] = trade(*result[2:4])
    outs = ()
    inner, outer = [None] * groups, [None] * groups
    for step in range(1, steps - 1, 2):
        width = 2 * REACH if step + 2 < steps - 1 else REACH
        for g in everyone:
            now[g], before[g], even, odd = pair_round(step, width, now[g], before[g], halos[g], courant, inject[g], along_z, along_y)
            halos[g] = trade(even, odd)
            if width == REACH:
                inner[g], *outs = inner_round(g, groups, steps - 1, now[g], before[g], courant, inject[g], along_z, along_y, outs)

    swap = [(i, i ^ 1) for i in range(shot_devices)]
    pairs = shot_devices // 2

    def travel(parts):
        sums = []
        for ahead, part in enumerate(parts, 1):
            route = [(2 * p + c, 2 * ((p + ahead) % pairs) + c) for p in range(pairs) for c in range(2)]
            sums.append(lax.ppermute(part, "shot", route))
        return sums

    def traded(fields):
        others = []
        for g in everyone:
            others.append(lax.ppermute(fields[g], "shot", swap))
        return fields + others

    inner = traded(inner)
    parts = [image_part(ahead, slots, offset_perm, inner) for ahead in range(1, pairs)]
    inner_sums = travel(parts)
    for g in everyone:
        outer[g], *outs = outer_round(g, steps - 1, now[g], before[g], halos[g], courant, inject[g], along_z, along_y, outs)
    outer = traded(outer)
    outer_sums = travel([image_part(ahead, slots, offset_perm, outer) for ahead in range(1, pairs)])
    image, own = inner_image(slots, rows, offset_perm, inner, outer, inner_sums)
    image = outer_image(image, own, outer_sums)
    return (image, *outs)


def solution(mesh):
    shots = ("runs", "shot")
    in_specs = (
        P(shots, "slab", None, None),
        P(shots, "slab", None, None),
        P(shots, "slab", None, None),
        P(shots, "slab", None, None),
        P(("runs", "slab"), None, None),
        P(shots),
        P(None, shots),
        P(shots, None),
        P(None, shots, None),
        P("runs"),
    )
    out_specs = (P(shots, "slab", None, None),) * 3
    return jax.shard_map(program, mesh=mesh, in_specs=in_specs, out_specs=out_specs, check_vma=False)
```

```python
import functools

import jax
import jax.numpy as jnp
from jax import lax
from jax.experimental import pallas as pl
from jax.experimental.pallas import tpu as pltpu
from jax.sharding import PartitionSpec as P


REACH = 4
INJECT_Z = 4
LANES = 128
CHUNK = 8

SCALE = 8.0 / 5.0
SIDE = 1.0 / 16.0
OWN = (1.0 + 2.0 * SIDE) * (-205.0 / 72.0) / SCALE
TAPS = (1.0, -1.0 / 8.0, 1.0 / 63.0, -1.0 / 896.0)

VMEM_LIMIT = 24 * 1024 * 1024


def vmem():
    return pl.BlockSpec(memory_space=pltpu.VMEM)


def smem():
    return pl.BlockSpec(memory_space=pltpu.SMEM)


def hbm():
    return pl.BlockSpec(memory_space=pltpu.HBM)


def params():
    return pltpu.CompilerParams(vmem_limit_bytes=VMEM_LIMIT)


def struct(shape, dtype=jnp.float32):
    return jax.ShapeDtypeStruct(shape, dtype)


def even_pairs(count):
    pairs = []
    for i in range(0, count - 1, 2):
        pairs += [(i, i + 1), (i + 1, i)]
    return pairs


def odd_pairs(count):
    pairs = []
    for i in range(1, count - 1, 2):
        pairs += [(i, i + 1), (i + 1, i)]
    return pairs


def trade(even_edge, odd_edge):
    count = lax.axis_size("slab")
    even = lax.ppermute(even_edge, "slab", even_pairs(count))
    odd = lax.ppermute(odd_edge, "slab", odd_pairs(count))
    return even, odd


def parity():
    return lax.rem(lax.axis_index("slab"), 2)


def edge_starts(rows, width):
    odd = parity()
    return (1 - odd) * (rows - width), odd * (rows - width)


def halo_starts(rows, width):
    odd = parity()
    return (1 - odd) * (rows + width), odd * (rows + width)


def pack_kernel(source, receiver, courant, even_edge, odd_edge, sem):
    groups, rows = source.shape[:2]
    copies = []
    for out, start in zip((even_edge, odd_edge), edge_starts(rows, REACH)):
        planes = pl.ds(start, REACH)
        pieces = [array.at[group, planes] for group in range(groups) for array in (source, receiver)]
        pieces.append(courant.at[planes])
        for index, piece in enumerate(pieces):
            copies.append(pltpu.make_async_copy(piece, out.at[index], sem.at[len(copies)]))
    for copy in copies:
        copy.start()
    for copy in copies:
        copy.wait()


def stay(*arrays):
    return [pltpu.with_memory_space_constraint(array, pltpu.HBM) for array in arrays]


def pack(source_now, receiver_now, courant_sq):
    groups, _, size_y, size_z = source_now.shape
    count = 2 * groups + 1
    return pl.pallas_call(
        pack_kernel,
        out_shape=[struct((count, REACH, size_y, size_z))] * 2,
        in_specs=[hbm()] * 3,
        out_specs=[vmem()] * 2,
        scratch_shapes=[pltpu.SemaphoreType.DMA((2 * count,))],
        compiler_params=params(),
        name="pack",
    )(*stay(source_now, receiver_now, courant_sq))


def band(distance):
    value = jnp.zeros(distance.shape, jnp.float32)
    for step, tap in enumerate(TAPS):
        value = jnp.where(distance == step + 1, SIDE * tap, value)
    return value


def prepare_kernel(groups, rows, source_cell, wavelet, receiver_cell, traces, source, receiver, source_before, receiver_before, along_z, along_y, *refs):
    planes, now, before, sem = refs[:groups], refs[groups : 2 * groups], refs[2 * groups : 3 * groups], refs[-1]
    copies = []
    for group in range(groups):
        pieces = ((source, now, 0), (receiver, now, 1), (source_before, before, 0), (receiver_before, before, 1))
        for array, place, kind in pieces:
            copies.append(pltpu.make_async_copy(array.at[group], place[group].at[kind], sem.at[len(copies)]))
    for copy in copies:
        copy.start()
    _, plane_count, size_y, _ = planes[0].shape
    steps = traces.shape[0]
    size_z = along_z.shape[0]
    block = along_y.shape[0]
    row = lax.broadcasted_iota(jnp.int32, (size_z, size_z), 0)
    col = lax.broadcasted_iota(jnp.int32, (size_z, size_z), 1)
    along_z[...] = band(jnp.abs(row - col)).astype(jnp.bfloat16)
    row = lax.broadcasted_iota(jnp.int32, (block, block), 0)
    col = lax.broadcasted_iota(jnp.int32, (block, block), 1)
    same = lax.div(row, size_y) == lax.div(col, size_y)
    half = jnp.where(same, band(jnp.abs(row - col)), 0.0).astype(jnp.bfloat16)
    along_y[:, :block] = half
    along_y[:, block:] = half
    first = (lax.axis_index("slab") * rows - REACH) * size_y
    cells = plane_count * size_y
    lane = lax.broadcasted_iota(jnp.int32, (1, LANES), 1)
    for group in range(groups):
        ids = first + lax.broadcasted_iota(jnp.int32, (cells, 1), 0)
        amplitude = jnp.zeros((1, LANES), jnp.float32)
        for step in range(steps):
            amplitude = jnp.where(lane == step, wavelet[step, group], amplitude)
        hit = jnp.broadcast_to(ids, (cells, LANES)) == source_cell[group]
        spread = jnp.where(hit, jnp.broadcast_to(amplitude, (cells, LANES)), 0.0)
        planes[group][0] = spread.reshape(plane_count, size_y, LANES)
        count = receiver_cell.shape[1]
        wide = first + lax.broadcasted_iota(jnp.int32, (cells, count), 0)
        here = jnp.broadcast_to(receiver_cell[group : group + 1, :], (cells, count))
        hot = (wide == here).astype(jnp.float32)
        data = traces[:, group, :]
        data = jnp.concatenate([data, jnp.zeros((LANES - steps, count), jnp.float32)], axis=0)
        summed = lax.dot_general(
            hot,
            data,
            (((1,), (1,)), ((), ())),
            precision=lax.Precision.HIGHEST,
            preferred_element_type=jnp.float32,
        )
        planes[group][1] = summed.reshape(plane_count, size_y, LANES)
    for copy in copies:
        copy.wait()


def prepare(source_cell, wavelet, receiver_cell, traces, fields):
    groups, rows, size_y, size_z = fields[0].shape
    block = CHUNK * size_y
    return pl.pallas_call(
        functools.partial(prepare_kernel, groups, rows),
        out_shape=[
            struct((size_z, size_z), jnp.bfloat16),
            struct((block, 2 * block), jnp.bfloat16),
        ]
        + [struct((2, rows + 2 * REACH, size_y, LANES))] * groups
        + [struct((2, rows, size_y, size_z))] * (2 * groups),
        in_specs=[smem(), smem(), vmem(), vmem()] + [hbm()] * 4,
        out_specs=[vmem()] * (2 + 3 * groups),
        scratch_shapes=[pltpu.SemaphoreType.DMA((4 * groups,))],
        compiler_params=params(),
        name="prepare",
    )(source_cell, wavelet, receiver_cell, traces, *stay(*fields))


def advance(now, at, before, before_at, courant, courant_at, inject, inject_at, runs, step, along_z, along_y, write):
    size_y, size_z = now.shape[-2:]
    pieces = [now[at + first : at + first + count].reshape(count * size_y, size_z) for first, count in runs]
    value = pieces[0] if len(pieces) == 1 else jnp.concatenate(pieces, axis=0)
    high = value.astype(jnp.bfloat16)
    low = (value - high.astype(jnp.float32)).astype(jnp.bfloat16)
    dot = functools.partial(jnp.dot, preferred_element_type=jnp.float32)
    sides = dot(high, along_z) + dot(low, along_z)
    sides = sides + dot(along_y, jnp.concatenate([high, low], axis=0))
    lane = lax.broadcasted_iota(jnp.int32, (size_y, LANES), 1)
    for i, plane in enumerate(first + j for first, count in runs for j in range(count)):
        here = at + plane
        own = now[here]
        total = sides[i * size_y : (i + 1) * size_y] + OWN * own
        for distance, tap in enumerate(TAPS, 1):
            pair = now[here + distance] + now[here - distance]
            total = total + (pair if tap == 1.0 else tap * pair)
        new = (own + own) - before[before_at + plane] + courant[courant_at + plane] * total
        spot = pltpu.roll(inject[inject_at + plane], (INJECT_Z - step) % LANES, 1)
        near = new[:, :LANES] + jnp.where(lane == INJECT_Z, spot, 0.0)
        write(i, plane, jnp.concatenate([near, new[:, LANES:]], axis=1))


def chunks(start, stop):
    return [[(at, CHUNK)] for at in range(start, stop, CHUNK)]


def first_kernel(group, rows, has_courant, width, now, before, courant, even, odd, inject, along_z, along_y, fresh, held, even_edge, odd_edge, *scaled):
    even_at, odd_at = halo_starts(rows, REACH)
    if has_courant:
        (courant_out,) = scaled
        courant_out[REACH : REACH + rows] = SCALE * courant[...]
        courant_out[pl.ds(even_at, REACH)] = SCALE * even[even.shape[0] - 1]
        courant_out[pl.ds(odd_at, REACH)] = SCALE * odd[odd.shape[0] - 1]
        courant = courant_out
    z_band, y_band = along_z[...], along_y[...]
    for kind in range(2):
        field = held.at[kind]
        field[REACH : REACH + rows] = now[kind]
        field[pl.ds(even_at, REACH)] = even[2 * group + kind]
        field[pl.ds(odd_at, REACH)] = odd[2 * group + kind]

        def write(i, plane, new, kind=kind):
            fresh[kind, plane] = new

        for runs in chunks(0, rows):
            advance(field, REACH, before.at[kind], 0, courant, REACH, inject.at[kind], REACH, runs, 0, z_band, y_band, write)
    send(rows, width, fresh, even_edge, odd_edge)


def send(rows, width, fresh, even_edge, odd_edge):
    even_from, odd_from = edge_starts(rows, width)
    even_edge[...] = fresh[:, pl.ds(even_from, width)]
    odd_edge[...] = fresh[:, pl.ds(odd_from, width)]


def first_round(group, width, now, before, courant, halos, inject, along_z, along_y):
    rows, size_y, size_z = now.shape[1:]
    has_courant = group == 0
    edge = struct((2, width, size_y, size_z))
    shapes = [struct(now.shape), struct((2, rows + 2 * REACH, size_y, size_z)), edge, edge]
    if has_courant:
        shapes.append(struct((rows + 2 * REACH, size_y, size_z)))
    return pl.pallas_call(
        functools.partial(first_kernel, group, rows, has_courant, width),
        out_shape=shapes,
        in_specs=[vmem()] * 8,
        out_specs=[vmem()] * len(shapes),
        compiler_params=params(),
    )(now, before, courant, *halos, inject, along_z, along_y)


def pair_kernel(rows, step, width, now, before, even, odd, courant, inject, along_z, along_y, fresh, held, even_edge, odd_edge, wide):
    reach = 2 * REACH
    even_at, odd_at = halo_starts(rows, reach)
    z_band, y_band = along_z[...], along_y[...]
    for kind in range(2):
        field = wide.at[kind]
        field[reach : reach + rows] = now[kind]
        field[pl.ds(even_at, reach)] = even[kind]
        field[pl.ds(odd_at, reach)] = odd[kind]
        middle = held.at[kind]

        def write_middle(i, plane, new, kind=kind):
            held[kind, REACH + plane] = new

        def write(i, plane, new, kind=kind):
            fresh[kind, plane] = new

        for runs in chunks(-REACH, rows + REACH):
            advance(field, reach, before.at[kind], REACH, courant, REACH, inject.at[kind], REACH, runs, step, z_band, y_band, write_middle)
        for runs in chunks(0, rows):
            advance(middle, REACH, field, reach, courant, REACH, inject.at[kind], REACH, runs, step + 1, z_band, y_band, write)
    send(rows, width, fresh, even_edge, odd_edge)


def pair_round(step, width, now, before, halos, courant, inject, along_z, along_y):
    rows, size_y, size_z = now.shape[1:]
    edge = struct((2, width, size_y, size_z))
    shapes = [struct(now.shape), struct((2, rows + 2 * REACH, size_y, size_z)), edge, edge]
    return pl.pallas_call(
        functools.partial(pair_kernel, rows, step, width),
        out_shape=shapes,
        in_specs=[vmem()] * 8,
        out_specs=[vmem()] * 4,
        scratch_shapes=[pltpu.VMEM((2, rows + 4 * REACH, size_y, size_z), jnp.float32)],
        compiler_params=params(),
    )(now, before, *halos, courant, inject, along_z, along_y)


def inner_kernel(groups, rows, step, *refs):
    now, before, inject = refs[:groups], refs[groups : 2 * groups], refs[2 * groups : 3 * groups]
    courant, along_z, along_y, final = refs[3 * groups :]
    z_band, y_band = along_z[...], along_y[...]
    for group in range(groups):
        for kind in range(2):

            def write(i, plane, new, place=2 * group + kind):
                final[place, plane - REACH] = new

            for runs in chunks(REACH, rows - REACH):
                advance(now[group].at[kind], 0, before[group].at[kind], REACH, courant, REACH, inject[group].at[kind], REACH, runs, step, z_band, y_band, write)


def inner_round(step, now, before, courant, inject, along_z, along_y):
    groups = len(now)
    rows, size_y, size_z = now[0].shape[1:]
    return pl.pallas_call(
        functools.partial(inner_kernel, groups, rows, step),
        out_shape=struct((2 * groups, rows - 2 * REACH, size_y, size_z)),
        in_specs=[vmem()] * (3 * groups + 3),
        out_specs=vmem(),
        compiler_params=params(),
        name="inner",
    )(*now, *before, *inject, courant, along_z, along_y)


def outer_kernel(groups, rows, step, *refs):
    now, before, inject = refs[:groups], refs[groups : 2 * groups], refs[2 * groups : 3 * groups]
    even, odd = refs[3 * groups : 4 * groups], refs[4 * groups : 5 * groups]
    courant, along_z, along_y, final, wide = refs[5 * groups :]
    even_at, odd_at = halo_starts(rows, REACH)
    z_band, y_band = along_z[...], along_y[...]
    for group in range(groups):
        for kind in range(2):
            field = wide.at[2 * group + kind]
            field[REACH : REACH + rows] = now[group][kind]
            field[pl.ds(even_at, REACH)] = even[group][kind]
            field[pl.ds(odd_at, REACH)] = odd[group][kind]

            def write(i, plane, new, place=2 * group + kind):
                final[place, i] = new

            runs = [(0, REACH), (rows - REACH, REACH)]
            advance(field, REACH, before[group].at[kind], REACH, courant, REACH, inject[group].at[kind], REACH, runs, step, z_band, y_band, write)


def outer_round(step, now, before, halos, courant, inject, along_z, along_y):
    groups = len(now)
    rows, size_y, size_z = now[0].shape[1:]
    even, odd = zip(*halos)
    return pl.pallas_call(
        functools.partial(outer_kernel, groups, rows, step),
        out_shape=struct((2 * groups, 2 * REACH, size_y, size_z)),
        in_specs=[vmem()] * (5 * groups + 3),
        out_specs=vmem(),
        scratch_shapes=[pltpu.VMEM((2 * groups, rows + 2 * REACH, size_y, size_z), jnp.float32)],
        compiler_params=params(),
        name="outer",
    )(*now, *before, *inject, *even, *odd, courant, along_z, along_y)


def shifted(plane, amount):
    size_y = plane.shape[0]
    if amount == 0:
        return plane
    if abs(amount) >= size_y:
        return jnp.zeros_like(plane)
    row = lax.broadcasted_iota(jnp.int32, plane.shape, 0)
    inside = (row >= amount) if amount > 0 else (row < size_y + amount)
    return jnp.where(inside, pltpu.roll(plane, amount % size_y, 0), 0.0)


def partial_image(ahead, offset_perm, fields, image, others=()):
    count = offset_perm.shape[0]
    half_span = count // 2
    slots, rows = image.shape[:2]
    here = lax.axis_index("shot")
    pairs = lax.axis_size("shot") // 2
    owner = 2 * lax.rem(lax.div(here, 2) + ahead, pairs) + lax.rem(here, 2)

    def one_slot(slot, carry):
        index = offset_perm[owner * slots + slot]
        for lag_index in range(count):
            lag = lag_index - half_span

            @pl.when(index == lag_index)
            def _(lag=lag):
                def one_plane(x, carry):
                    total = None
                    for field in fields:
                        for source in range(0, field.shape[0], 2):
                            term = field[source + 1, x] * shifted(field[source, x], 2 * lag)
                            total = term if total is None else total + term
                    total = shifted(total, -lag)
                    for other in others:
                        total = total + other[slot, x]
                    image[slot, x] = total
                    return carry

                lax.fori_loop(0, rows, one_plane, 0, unroll=4)

        return carry

    lax.fori_loop(0, slots, one_slot, 0)


def image_kernel(ahead, offset_perm, *refs):
    partial_image(ahead, offset_perm, refs[:-1], refs[-1])


def image_part(ahead, slots, offset_perm, fields):
    _, rows, size_y, size_z = fields[0].shape
    return pl.pallas_call(
        functools.partial(image_kernel, ahead),
        out_shape=struct((slots, rows, size_y, size_z)),
        in_specs=[smem()] + [vmem()] * len(fields),
        out_specs=vmem(),
        compiler_params=params(),
    )(offset_perm, *fields)


def inner_image_kernel(offset_perm, own_inner, other_inner, own_outer, other_outer, *refs):
    others = refs[:-6]
    image, source_out, receiver_out, outer, inner, sem = refs[-6:]
    groups, rows = source_out.shape[:2]
    copies = []
    for group in range(groups):
        for kind, out in enumerate((source_out, receiver_out)):
            place = 2 * group + kind
            pieces = (
                (own_inner.at[place], REACH, rows - 2 * REACH),
                (own_outer.at[place, pl.ds(0, REACH)], 0, REACH),
                (own_outer.at[place, pl.ds(REACH, REACH)], rows - REACH, REACH),
            )
            for piece, first, count in pieces:
                copies.append(pltpu.make_async_copy(piece, out.at[group, pl.ds(first, count)], sem.at[len(copies)]))
                copies[-1].start()
    partial_image(0, offset_perm, (own_inner, other_inner), inner, others)
    copies.append(pltpu.make_async_copy(inner, image.at[:, pl.ds(REACH, rows - 2 * REACH)], sem.at[len(copies)]))
    copies[-1].start()
    partial_image(0, offset_perm, (own_outer, other_outer), outer)
    for copy in copies:
        copy.wait()


def inner_image(slots, inner, outer, others, offset_perm):
    places, inner_rows, size_y, size_z = inner[0].shape
    rows = inner_rows + 2 * REACH
    whole = struct((places // 2, rows, size_y, size_z))
    return pl.pallas_call(
        inner_image_kernel,
        out_shape=[struct((slots, rows, size_y, size_z)), whole, whole, struct((slots, 2 * REACH, size_y, size_z))],
        in_specs=[smem()] + [vmem()] * (4 + len(others)),
        out_specs=[hbm()] * 3 + [vmem()],
        scratch_shapes=[pltpu.VMEM((slots, inner_rows, size_y, size_z), jnp.float32), pltpu.SemaphoreType.DMA((3 * places + 1,))],
        compiler_params=params(),
        name="image_inner",
    )(offset_perm, *inner, *outer, *others)


def outer_image_kernel(rows, *refs):
    own, others = refs[0], refs[1:-4]
    image, outer, sem = refs[-3:]
    copies = []
    for side, first in enumerate((0, rows - REACH)):
        planes = pl.ds(side * REACH, REACH)
        total = own[:, planes]
        for other in others:
            total = total + other[:, planes]
        outer[:, planes] = total
        copies.append(pltpu.make_async_copy(outer.at[:, planes], image.at[:, pl.ds(first, REACH)], sem.at[side]))
        copies[side].start()
    for copy in copies:
        copy.wait()


def outer_image(image, own, others):
    return pl.pallas_call(
        functools.partial(outer_image_kernel, image.shape[1]),
        out_shape=struct(image.shape),
        in_specs=[vmem()] * (1 + len(others)) + [hbm()],
        out_specs=hbm(),
        scratch_shapes=[pltpu.VMEM(own.shape, jnp.float32), pltpu.SemaphoreType.DMA((2,))],
        input_output_aliases={1 + len(others): 0},
        compiler_params=params(),
        name="image_outer",
    )(own, *others, image)


def program(source_now, source_prev, receiver_now, receiver_prev, courant_sq, source_cell, wavelet, receiver_cell, traces, offset_perm):
    groups, _, _, _ = source_now.shape
    steps = wavelet.shape[0]
    shot_devices = lax.axis_size("shot")
    slots = offset_perm.shape[0] // shot_devices
    everyone = range(groups)

    given = trade(*pack(source_now, receiver_now, courant_sq))
    fields = (source_now, receiver_now, source_prev, receiver_prev)
    along_z, along_y, *rest = prepare(source_cell, wavelet, receiver_cell, traces, fields)
    inject, now, before = rest[:groups], rest[groups : 2 * groups], rest[2 * groups :]

    halos = [None] * groups
    courant = courant_sq
    for g in everyone:
        result = first_round(g, 2 * REACH, now[g], before[g], courant, given, inject[g], along_z, along_y)
        now[g], before[g] = result[:2]
        if g == 0:
            courant = result[4]
        halos[g] = trade(*result[2:4])
    for step in range(1, steps - 1, 2):
        last = step + 2 >= steps - 1
        for g in everyone:
            now[g], before[g], even, odd = pair_round(step, REACH if last else 2 * REACH, now[g], before[g], halos[g], courant, inject[g], along_z, along_y)
            halos[g] = trade(even, odd)

    swap = [(i, i ^ 1) for i in range(shot_devices)]
    pairs = shot_devices // 2

    def part_sums(fields):
        parts = [image_part(ahead, slots, offset_perm, fields) for ahead in range(1, pairs)]
        sums = []
        for ahead, part in enumerate(parts, 1):
            route = [(2 * p + c, 2 * ((p + ahead) % pairs) + c) for p in range(pairs) for c in range(2)]
            sums.append(lax.ppermute(part, "shot", route))
        return sums

    own = inner_round(steps - 1, now, before, courant, inject, along_z, along_y)
    inner = (own, lax.ppermute(own, "shot", swap))
    inner_sums = part_sums(inner)
    own = outer_round(steps - 1, now, before, halos, courant, inject, along_z, along_y)
    outer = (own, lax.ppermute(own, "shot", swap))
    outer_sums = part_sums(outer)
    image, source_final, receiver_final, own = inner_image(slots, inner, outer, inner_sums, offset_perm)
    image = outer_image(image, own, outer_sums)
    return image, source_final, receiver_final


def solution(mesh):
    shots = ("runs", "shot")
    in_specs = (
        P(shots, "slab", None, None),
        P(shots, "slab", None, None),
        P(shots, "slab", None, None),
        P(shots, "slab", None, None),
        P(("runs", "slab"), None, None),
        P(shots),
        P(None, shots),
        P(shots, None),
        P(None, shots, None),
        P("runs"),
    )
    out_specs = (P(shots, "slab", None, None),) * 3
    return jax.shard_map(program, mesh=mesh, in_specs=in_specs, out_specs=out_specs, check_vma=False)
```

```python
import functools

import jax
import jax.numpy as jnp
from jax import lax
from jax.experimental import pallas as pl
from jax.experimental.pallas import tpu as pltpu
from jax.sharding import PartitionSpec as P


REACH = 4
INJECT_Z = 4
LANES = 128
CHUNK = 8

SCALE = 8.0 / 5.0
SIDE = 1.0 / 16.0
OWN = (1.0 + 2.0 * SIDE) * (-205.0 / 72.0) / SCALE
TAPS = (1.0, -1.0 / 8.0, 1.0 / 63.0, -1.0 / 896.0)

VMEM_LIMIT = 24 * 1024 * 1024


def vmem():
    return pl.BlockSpec(memory_space=pltpu.VMEM)


def smem():
    return pl.BlockSpec(memory_space=pltpu.SMEM)


def hbm():
    return pl.BlockSpec(memory_space=pltpu.HBM)


def params():
    return pltpu.CompilerParams(vmem_limit_bytes=VMEM_LIMIT)


def struct(shape, dtype=jnp.float32):
    return jax.ShapeDtypeStruct(shape, dtype)


def even_pairs(count):
    pairs = []
    for i in range(0, count - 1, 2):
        pairs += [(i, i + 1), (i + 1, i)]
    return pairs


def odd_pairs(count):
    pairs = []
    for i in range(1, count - 1, 2):
        pairs += [(i, i + 1), (i + 1, i)]
    return pairs


def trade(even_edge, odd_edge):
    count = lax.axis_size("slab")
    even = lax.ppermute(even_edge, "slab", even_pairs(count))
    odd = lax.ppermute(odd_edge, "slab", odd_pairs(count))
    return even, odd


def parity():
    return lax.rem(lax.axis_index("slab"), 2)


def edge_starts(rows, width):
    odd = parity()
    return (1 - odd) * (rows - width), odd * (rows - width)


def halo_starts(rows, width):
    odd = parity()
    return (1 - odd) * (rows + width), odd * (rows + width)


def pack_kernel(source, receiver, courant, *refs):
    groups, rows = source.shape[:2]
    outs, sem = refs[:-1], refs[-1]
    copies = []
    for group in range(groups):
        for side, start in enumerate(edge_starts(rows, REACH)):
            planes = pl.ds(start, REACH)
            pieces = [source.at[group, planes], receiver.at[group, planes]]
            if group == 0:
                pieces.append(courant.at[planes])
            for index, piece in enumerate(pieces):
                copies.append(pltpu.make_async_copy(piece, outs[2 * group + side].at[index], sem.at[len(copies)]))
    for copy in copies:
        copy.start()
    for copy in copies:
        copy.wait()


def stay(*arrays):
    return [pltpu.with_memory_space_constraint(array, pltpu.HBM) for array in arrays]


def pack(source_now, receiver_now, courant_sq):
    groups, _, size_y, size_z = source_now.shape
    shapes = [struct((3 if group == 0 else 2, REACH, size_y, size_z)) for group in range(groups) for _ in range(2)]
    return pl.pallas_call(
        pack_kernel,
        out_shape=shapes,
        in_specs=[hbm()] * 3,
        out_specs=[vmem()] * len(shapes),
        scratch_shapes=[pltpu.SemaphoreType.DMA((4 * groups + 2,))],
        compiler_params=params(),
        name="pack",
    )(*stay(source_now, receiver_now, courant_sq))


def band(distance):
    value = jnp.zeros(distance.shape, jnp.float32)
    for step, tap in enumerate(TAPS):
        value = jnp.where(distance == step + 1, SIDE * tap, value)
    return value


def prepare_kernel(groups, rows, source_cell, wavelet, receiver_cell, traces, source, receiver, source_before, receiver_before, along_z, along_y, *refs):
    planes, now, before, sem = refs[:groups], refs[groups : 2 * groups], refs[2 * groups : 3 * groups], refs[-1]
    copies = []
    for group in range(groups):
        pieces = ((source, now, 0), (receiver, now, 1), (source_before, before, 0), (receiver_before, before, 1))
        for array, place, kind in pieces:
            copies.append(pltpu.make_async_copy(array.at[group], place[group].at[kind], sem.at[len(copies)]))
    for copy in copies:
        copy.start()
    _, plane_count, size_y, _ = planes[0].shape
    steps = traces.shape[0]
    size_z = along_z.shape[0]
    block = along_y.shape[0]
    row = lax.broadcasted_iota(jnp.int32, (size_z, size_z), 0)
    col = lax.broadcasted_iota(jnp.int32, (size_z, size_z), 1)
    along_z[...] = band(jnp.abs(row - col)).astype(jnp.bfloat16)
    row = lax.broadcasted_iota(jnp.int32, (block, block), 0)
    col = lax.broadcasted_iota(jnp.int32, (block, block), 1)
    same = lax.div(row, size_y) == lax.div(col, size_y)
    half = jnp.where(same, band(jnp.abs(row - col)), 0.0).astype(jnp.bfloat16)
    along_y[:, :block] = half
    along_y[:, block:] = half
    first = (lax.axis_index("slab") * rows - REACH) * size_y
    cells = plane_count * size_y
    lane = lax.broadcasted_iota(jnp.int32, (1, LANES), 1)
    for group in range(groups):
        ids = first + lax.broadcasted_iota(jnp.int32, (cells, 1), 0)
        amplitude = jnp.zeros((1, LANES), jnp.float32)
        for step in range(steps):
            amplitude = jnp.where(lane == step, wavelet[step, group], amplitude)
        hit = jnp.broadcast_to(ids, (cells, LANES)) == source_cell[group]
        spread = jnp.where(hit, jnp.broadcast_to(amplitude, (cells, LANES)), 0.0)
        planes[group][0] = spread.reshape(plane_count, size_y, LANES)
        count = receiver_cell.shape[1]
        wide = first + lax.broadcasted_iota(jnp.int32, (cells, count), 0)
        here = jnp.broadcast_to(receiver_cell[group : group + 1, :], (cells, count))
        hot = (wide == here).astype(jnp.float32)
        data = traces[:, group, :]
        data = jnp.concatenate([data, jnp.zeros((LANES - steps, count), jnp.float32)], axis=0)
        summed = lax.dot_general(
            hot,
            data,
            (((1,), (1,)), ((), ())),
            precision=lax.Precision.HIGHEST,
            preferred_element_type=jnp.float32,
        )
        planes[group][1] = summed.reshape(plane_count, size_y, LANES)
    for copy in copies:
        copy.wait()


def prepare(source_cell, wavelet, receiver_cell, traces, fields):
    groups, rows, size_y, size_z = fields[0].shape
    block = CHUNK * size_y
    return pl.pallas_call(
        functools.partial(prepare_kernel, groups, rows),
        out_shape=[
            struct((size_z, size_z), jnp.bfloat16),
            struct((block, 2 * block), jnp.bfloat16),
        ]
        + [struct((2, rows + 2 * REACH, size_y, LANES))] * groups
        + [struct((2, rows, size_y, size_z))] * (2 * groups),
        in_specs=[smem(), smem(), vmem(), vmem()] + [hbm()] * 4,
        out_specs=[vmem()] * (2 + 3 * groups),
        scratch_shapes=[pltpu.SemaphoreType.DMA((4 * groups,))],
        compiler_params=params(),
        name="prepare",
    )(source_cell, wavelet, receiver_cell, traces, *stay(*fields))


def advance(now, at, before, before_at, courant, courant_at, inject, inject_at, runs, step, along_z, along_y, write):
    size_y, size_z = now.shape[-2:]
    pieces = [now[at + first : at + first + count].reshape(count * size_y, size_z) for first, count in runs]
    value = pieces[0] if len(pieces) == 1 else jnp.concatenate(pieces, axis=0)
    high = value.astype(jnp.bfloat16)
    low = (value - high.astype(jnp.float32)).astype(jnp.bfloat16)
    dot = functools.partial(jnp.dot, preferred_element_type=jnp.float32)
    sides = dot(high, along_z) + dot(low, along_z)
    sides = sides + dot(along_y, jnp.concatenate([high, low], axis=0))
    lane = lax.broadcasted_iota(jnp.int32, (size_y, LANES), 1)
    for i, plane in enumerate(first + j for first, count in runs for j in range(count)):
        here = at + plane
        own = now[here]
        total = sides[i * size_y : (i + 1) * size_y] + OWN * own
        for distance, tap in enumerate(TAPS, 1):
            pair = now[here + distance] + now[here - distance]
            total = total + (pair if tap == 1.0 else tap * pair)
        new = (own + own) - before[before_at + plane] + courant[courant_at + plane] * total
        spot = pltpu.roll(inject[inject_at + plane], (INJECT_Z - step) % LANES, 1)
        near = new[:, :LANES] + jnp.where(lane == INJECT_Z, spot, 0.0)
        write(i, plane, jnp.concatenate([near, new[:, LANES:]], axis=1))


def chunks(start, stop):
    return [[(at, CHUNK)] for at in range(start, stop, CHUNK)]


def first_kernel(rows, has_courant, width, now, before, courant, even, odd, inject, along_z, along_y, fresh, held, even_edge, odd_edge, *scaled):
    even_at, odd_at = halo_starts(rows, REACH)
    if has_courant:
        (courant_out,) = scaled
        courant_out[REACH : REACH + rows] = SCALE * courant[...]
        courant_out[pl.ds(even_at, REACH)] = SCALE * even[2]
        courant_out[pl.ds(odd_at, REACH)] = SCALE * odd[2]
        courant = courant_out
    z_band, y_band = along_z[...], along_y[...]
    for kind in range(2):
        field = held.at[kind]
        field[REACH : REACH + rows] = now[kind]
        field[pl.ds(even_at, REACH)] = even[kind]
        field[pl.ds(odd_at, REACH)] = odd[kind]

        def write(i, plane, new, kind=kind):
            fresh[kind, plane] = new

        for runs in chunks(0, rows):
            advance(field, REACH, before.at[kind], 0, courant, REACH, inject.at[kind], REACH, runs, 0, z_band, y_band, write)
    send(rows, width, fresh, even_edge, odd_edge)


def send(rows, width, fresh, even_edge, odd_edge):
    even_from, odd_from = edge_starts(rows, width)
    even_edge[...] = fresh[:, pl.ds(even_from, width)]
    odd_edge[...] = fresh[:, pl.ds(odd_from, width)]


def first_round(group, width, now, before, courant, halos, inject, along_z, along_y):
    rows, size_y, size_z = now.shape[1:]
    has_courant = group == 0
    edge = struct((2, width, size_y, size_z))
    shapes = [struct(now.shape), struct((2, rows + 2 * REACH, size_y, size_z)), edge, edge]
    if has_courant:
        shapes.append(struct((rows + 2 * REACH, size_y, size_z)))
    return pl.pallas_call(
        functools.partial(first_kernel, rows, has_courant, width),
        out_shape=shapes,
        in_specs=[vmem()] * 8,
        out_specs=[vmem()] * len(shapes),
        compiler_params=params(),
    )(now, before, courant, *halos, inject, along_z, along_y)


def pair_kernel(rows, step, width, now, before, even, odd, courant, inject, along_z, along_y, fresh, held, even_edge, odd_edge, wide):
    reach = 2 * REACH
    even_at, odd_at = halo_starts(rows, reach)
    z_band, y_band = along_z[...], along_y[...]
    for kind in range(2):
        field = wide.at[kind]
        field[reach : reach + rows] = now[kind]
        field[pl.ds(even_at, reach)] = even[kind]
        field[pl.ds(odd_at, reach)] = odd[kind]
        middle = held.at[kind]

        def write_middle(i, plane, new, kind=kind):
            held[kind, REACH + plane] = new

        def write(i, plane, new, kind=kind):
            fresh[kind, plane] = new

        for runs in chunks(-REACH, rows + REACH):
            advance(field, reach, before.at[kind], REACH, courant, REACH, inject.at[kind], REACH, runs, step, z_band, y_band, write_middle)
        for runs in chunks(0, rows):
            advance(middle, REACH, field, reach, courant, REACH, inject.at[kind], REACH, runs, step + 1, z_band, y_band, write)
    send(rows, width, fresh, even_edge, odd_edge)


def pair_round(step, width, now, before, halos, courant, inject, along_z, along_y):
    rows, size_y, size_z = now.shape[1:]
    edge = struct((2, width, size_y, size_z))
    shapes = [struct(now.shape), struct((2, rows + 2 * REACH, size_y, size_z)), edge, edge]
    return pl.pallas_call(
        functools.partial(pair_kernel, rows, step, width),
        out_shape=shapes,
        in_specs=[vmem()] * 8,
        out_specs=[vmem()] * 4,
        scratch_shapes=[pltpu.VMEM((2, rows + 4 * REACH, size_y, size_z), jnp.float32)],
        compiler_params=params(),
    )(now, before, *halos, courant, inject, along_z, along_y)


def inner_kernel(groups, rows, step, *refs):
    now, before, inject = refs[:groups], refs[groups : 2 * groups], refs[2 * groups : 3 * groups]
    courant, along_z, along_y, final = refs[3 * groups :]
    z_band, y_band = along_z[...], along_y[...]
    for group in range(groups):
        for kind in range(2):

            def write(i, plane, new, place=2 * group + kind):
                final[place, plane - REACH] = new

            for runs in chunks(REACH, rows - REACH):
                advance(now[group].at[kind], 0, before[group].at[kind], REACH, courant, REACH, inject[group].at[kind], REACH, runs, step, z_band, y_band, write)


def inner_round(step, now, before, courant, inject, along_z, along_y):
    groups = len(now)
    rows, size_y, size_z = now[0].shape[1:]
    return pl.pallas_call(
        functools.partial(inner_kernel, groups, rows, step),
        out_shape=struct((2 * groups, rows - 2 * REACH, size_y, size_z)),
        in_specs=[vmem()] * (3 * groups + 3),
        out_specs=vmem(),
        compiler_params=params(),
        name="inner",
    )(*now, *before, *inject, courant, along_z, along_y)


def outer_kernel(groups, rows, step, *refs):
    now, before, inject = refs[:groups], refs[groups : 2 * groups], refs[2 * groups : 3 * groups]
    even, odd = refs[3 * groups : 4 * groups], refs[4 * groups : 5 * groups]
    courant, along_z, along_y, final, wide = refs[5 * groups :]
    even_at, odd_at = halo_starts(rows, REACH)
    z_band, y_band = along_z[...], along_y[...]
    for group in range(groups):
        for kind in range(2):
            field = wide.at[2 * group + kind]
            field[REACH : REACH + rows] = now[group][kind]
            field[pl.ds(even_at, REACH)] = even[group][kind]
            field[pl.ds(odd_at, REACH)] = odd[group][kind]

            def write(i, plane, new, place=2 * group + kind):
                final[place, i] = new

            runs = [(0, REACH), (rows - REACH, REACH)]
            advance(field, REACH, before[group].at[kind], REACH, courant, REACH, inject[group].at[kind], REACH, runs, step, z_band, y_band, write)


def outer_round(step, now, before, halos, courant, inject, along_z, along_y):
    groups = len(now)
    rows, size_y, size_z = now[0].shape[1:]
    even, odd = zip(*halos)
    return pl.pallas_call(
        functools.partial(outer_kernel, groups, rows, step),
        out_shape=struct((2 * groups, 2 * REACH, size_y, size_z)),
        in_specs=[vmem()] * (5 * groups + 3),
        out_specs=vmem(),
        scratch_shapes=[pltpu.VMEM((2 * groups, rows + 2 * REACH, size_y, size_z), jnp.float32)],
        compiler_params=params(),
        name="outer",
    )(*now, *before, *inject, *even, *odd, courant, along_z, along_y)


def shifted(plane, amount):
    size_y = plane.shape[0]
    if amount == 0:
        return plane
    if abs(amount) >= size_y:
        return jnp.zeros_like(plane)
    row = lax.broadcasted_iota(jnp.int32, plane.shape, 0)
    inside = (row >= amount) if amount > 0 else (row < size_y + amount)
    return jnp.where(inside, pltpu.roll(plane, amount % size_y, 0), 0.0)


def partial_image(ahead, offset_perm, fields, image, others=()):
    count = offset_perm.shape[0]
    half_span = count // 2
    slots, rows = image.shape[:2]
    here = lax.axis_index("shot")
    pairs = lax.axis_size("shot") // 2
    owner = 2 * lax.rem(lax.div(here, 2) + ahead, pairs) + lax.rem(here, 2)

    def one_slot(slot, carry):
        index = offset_perm[owner * slots + slot]
        for lag_index in range(count):
            lag = lag_index - half_span

            @pl.when(index == lag_index)
            def _(lag=lag):
                def one_plane(x, carry):
                    total = None
                    for field in fields:
                        for source in range(0, field.shape[0], 2):
                            term = field[source + 1, x] * shifted(field[source, x], 2 * lag)
                            total = term if total is None else total + term
                    total = shifted(total, -lag)
                    for other in others:
                        total = total + other[slot, x]
                    image[slot, x] = total
                    return carry

                lax.fori_loop(0, rows, one_plane, 0, unroll=4)

        return carry

    lax.fori_loop(0, slots, one_slot, 0)


def image_kernel(ahead, offset_perm, *refs):
    partial_image(ahead, offset_perm, refs[:-1], refs[-1])


def image_part(ahead, slots, offset_perm, fields):
    _, rows, size_y, size_z = fields[0].shape
    return pl.pallas_call(
        functools.partial(image_kernel, ahead),
        out_shape=struct((slots, rows, size_y, size_z)),
        in_specs=[smem()] + [vmem()] * len(fields),
        out_specs=vmem(),
        compiler_params=params(),
    )(offset_perm, *fields)


def inner_image_kernel(offset_perm, own_inner, other_inner, own_outer, other_outer, *refs):
    others = refs[:-6]
    image, source_out, receiver_out, outer, inner, sem = refs[-6:]
    groups, rows = source_out.shape[:2]
    copies = []
    for group in range(groups):
        for kind, out in enumerate((source_out, receiver_out)):
            place = 2 * group + kind
            pieces = (
                (own_inner.at[place], REACH, rows - 2 * REACH),
                (own_outer.at[place, pl.ds(0, REACH)], 0, REACH),
                (own_outer.at[place, pl.ds(REACH, REACH)], rows - REACH, REACH),
            )
            for piece, first, count in pieces:
                copies.append(pltpu.make_async_copy(piece, out.at[group, pl.ds(first, count)], sem.at[len(copies)]))
                copies[-1].start()
    partial_image(0, offset_perm, (own_inner, other_inner), inner, others)
    copies.append(pltpu.make_async_copy(inner, image.at[:, pl.ds(REACH, rows - 2 * REACH)], sem.at[len(copies)]))
    copies[-1].start()
    partial_image(0, offset_perm, (own_outer, other_outer), outer)
    for copy in copies:
        copy.wait()


def inner_image(slots, inner, outer, others, offset_perm):
    places, inner_rows, size_y, size_z = inner[0].shape
    rows = inner_rows + 2 * REACH
    whole = struct((places // 2, rows, size_y, size_z))
    return pl.pallas_call(
        inner_image_kernel,
        out_shape=[struct((slots, rows, size_y, size_z)), whole, whole, struct((slots, 2 * REACH, size_y, size_z))],
        in_specs=[smem()] + [vmem()] * (4 + len(others)),
        out_specs=[hbm()] * 3 + [vmem()],
        scratch_shapes=[pltpu.VMEM((slots, inner_rows, size_y, size_z), jnp.float32), pltpu.SemaphoreType.DMA((3 * places + 1,))],
        compiler_params=params(),
        name="image_inner",
    )(offset_perm, *inner, *outer, *others)


def outer_image_kernel(rows, *refs):
    own, others = refs[0], refs[1:-4]
    image, outer, sem = refs[-3:]
    copies = []
    for side, first in enumerate((0, rows - REACH)):
        planes = pl.ds(side * REACH, REACH)
        total = own[:, planes]
        for other in others:
            total = total + other[:, planes]
        outer[:, planes] = total
        copies.append(pltpu.make_async_copy(outer.at[:, planes], image.at[:, pl.ds(first, REACH)], sem.at[side]))
        copies[side].start()
    for copy in copies:
        copy.wait()


def outer_image(image, own, others):
    return pl.pallas_call(
        functools.partial(outer_image_kernel, image.shape[1]),
        out_shape=struct(image.shape),
        in_specs=[vmem()] * (1 + len(others)) + [hbm()],
        out_specs=hbm(),
        scratch_shapes=[pltpu.VMEM(own.shape, jnp.float32), pltpu.SemaphoreType.DMA((2,))],
        input_output_aliases={1 + len(others): 0},
        compiler_params=params(),
        name="image_outer",
    )(own, *others, image)


def program(source_now, source_prev, receiver_now, receiver_prev, courant_sq, source_cell, wavelet, receiver_cell, traces, offset_perm):
    groups, _, _, _ = source_now.shape
    steps = wavelet.shape[0]
    shot_devices = lax.axis_size("shot")
    slots = offset_perm.shape[0] // shot_devices
    everyone = range(groups)

    edges = pack(source_now, receiver_now, courant_sq)
    given = [trade(edges[2 * g], edges[2 * g + 1]) for g in everyone]
    fields = (source_now, receiver_now, source_prev, receiver_prev)
    along_z, along_y, *rest = prepare(source_cell, wavelet, receiver_cell, traces, fields)
    inject, now, before = rest[:groups], rest[groups : 2 * groups], rest[2 * groups :]

    halos = [None] * groups
    courant = courant_sq
    for g in everyone:
        result = first_round(g, 2 * REACH, now[g], before[g], courant, given[g], inject[g], along_z, along_y)
        now[g], before[g] = result[:2]
        if g == 0:
            courant = result[4]
        halos[g] = trade(*result[2:4])
    for step in range(1, steps - 1, 2):
        last = step + 2 >= steps - 1
        for g in everyone:
            now[g], before[g], even, odd = pair_round(step, REACH if last else 2 * REACH, now[g], before[g], halos[g], courant, inject[g], along_z, along_y)
            halos[g] = trade(even, odd)

    swap = [(i, i ^ 1) for i in range(shot_devices)]
    pairs = shot_devices // 2

    def part_sums(fields):
        parts = [image_part(ahead, slots, offset_perm, fields) for ahead in range(1, pairs)]
        sums = []
        for ahead, part in enumerate(parts, 1):
            route = [(2 * p + c, 2 * ((p + ahead) % pairs) + c) for p in range(pairs) for c in range(2)]
            sums.append(lax.ppermute(part, "shot", route))
        return sums

    own = inner_round(steps - 1, now, before, courant, inject, along_z, along_y)
    inner = (own, lax.ppermute(own, "shot", swap))
    inner_sums = part_sums(inner)
    own = outer_round(steps - 1, now, before, halos, courant, inject, along_z, along_y)
    outer = (own, lax.ppermute(own, "shot", swap))
    outer_sums = part_sums(outer)
    image, source_final, receiver_final, own = inner_image(slots, inner, outer, inner_sums, offset_perm)
    image = outer_image(image, own, outer_sums)
    return image, source_final, receiver_final


def solution(mesh):
    shots = ("runs", "shot")
    in_specs = (
        P(shots, "slab", None, None),
        P(shots, "slab", None, None),
        P(shots, "slab", None, None),
        P(shots, "slab", None, None),
        P(("runs", "slab"), None, None),
        P(shots),
        P(None, shots),
        P(shots, None),
        P(None, shots, None),
        P("runs"),
    )
    out_specs = (P(shots, "slab", None, None),) * 3
    return jax.shard_map(program, mesh=mesh, in_specs=in_specs, out_specs=out_specs, check_vma=False)
```

```python
import functools

import jax
import jax.numpy as jnp
from jax import lax
from jax.experimental import pallas as pl
from jax.experimental.pallas import tpu as pltpu
from jax.sharding import PartitionSpec as P


REACH = 4
INJECT_Z = 4
LANES = 128
CHUNK = 8

SCALE = 8.0 / 5.0
SIDE = 1.0 / 16.0
OWN = (1.0 + 2.0 * SIDE) * (-205.0 / 72.0) / SCALE
TAPS = (1.0, -1.0 / 8.0, 1.0 / 63.0, -1.0 / 896.0)

VMEM_LIMIT = 24 * 1024 * 1024


def vmem():
    return pl.BlockSpec(memory_space=pltpu.VMEM)


def smem():
    return pl.BlockSpec(memory_space=pltpu.SMEM)


def hbm():
    return pl.BlockSpec(memory_space=pltpu.HBM)


def params():
    return pltpu.CompilerParams(vmem_limit_bytes=VMEM_LIMIT)


def struct(shape, dtype=jnp.float32):
    return jax.ShapeDtypeStruct(shape, dtype)


def even_pairs(count):
    pairs = []
    for i in range(0, count - 1, 2):
        pairs += [(i, i + 1), (i + 1, i)]
    return pairs


def odd_pairs(count):
    pairs = []
    for i in range(1, count - 1, 2):
        pairs += [(i, i + 1), (i + 1, i)]
    return pairs


def trade(even_edge, odd_edge):
    count = lax.axis_size("slab")
    even = lax.ppermute(even_edge, "slab", even_pairs(count))
    odd = lax.ppermute(odd_edge, "slab", odd_pairs(count))
    return even, odd


def parity():
    return lax.rem(lax.axis_index("slab"), 2)


def edge_starts(rows, width):
    odd = parity()
    return (1 - odd) * (rows - width), odd * (rows - width)


def halo_starts(rows, width):
    odd = parity()
    return (1 - odd) * (rows + width), odd * (rows + width)


def pack_kernel(source, receiver, courant, *refs):
    groups, rows = source.shape[:2]
    outs, sem = refs[:-1], refs[-1]
    copies = []
    for group in range(groups):
        for side, start in enumerate(edge_starts(rows, REACH)):
            planes = pl.ds(start, REACH)
            pieces = [source.at[group, planes], receiver.at[group, planes]]
            if group == 0:
                pieces.append(courant.at[planes])
            for index, piece in enumerate(pieces):
                copies.append(pltpu.make_async_copy(piece, outs[2 * group + side].at[index], sem.at[len(copies)]))
    for copy in copies:
        copy.start()
    for copy in copies:
        copy.wait()


def stay(*arrays):
    return [pltpu.with_memory_space_constraint(array, pltpu.HBM) for array in arrays]


def pack(source_now, receiver_now, courant_sq):
    groups, _, size_y, size_z = source_now.shape
    shapes = [struct((3 if group == 0 else 2, REACH, size_y, size_z)) for group in range(groups) for _ in range(2)]
    return pl.pallas_call(
        pack_kernel,
        out_shape=shapes,
        in_specs=[hbm()] * 3,
        out_specs=[vmem()] * len(shapes),
        scratch_shapes=[pltpu.SemaphoreType.DMA((4 * groups + 2,))],
        compiler_params=params(),
        name="pack",
    )(*stay(source_now, receiver_now, courant_sq))


def band(distance):
    value = jnp.zeros(distance.shape, jnp.float32)
    for step, tap in enumerate(TAPS):
        value = jnp.where(distance == step + 1, SIDE * tap, value)
    return value


def fetch(pieces, sem):
    copies = [pltpu.make_async_copy(array, place, sem.at[index]) for index, (array, place) in enumerate(pieces)]
    for copy in copies:
        copy.start()
    return copies


def prepare_kernel(groups, rows, source_cell, wavelet, offset_perm, receiver_cell, traces, source, receiver, source_before, receiver_before, along_z, along_y, lags, *refs):
    planes, now, before, sem = refs[:groups], refs[groups : 2 * groups], refs[2 * groups : 3 * groups], refs[-1]
    pieces = []
    for group in range(groups):
        pieces += [(source.at[group], now[group].at[0]), (receiver.at[group], now[group].at[1])]
        pieces += [(source_before.at[group], before[group].at[0]), (receiver_before.at[group], before[group].at[1])]
    copies = fetch(pieces, sem)
    _, plane_count, size_y, _ = planes[0].shape
    steps = traces.shape[0]
    size_z = along_z.shape[0]
    block = along_y.shape[0]
    for slot in range(offset_perm.shape[0]):
        lags[slot : slot + 1, :] = jnp.full((1, LANES), offset_perm[slot], jnp.int32)
    row = lax.broadcasted_iota(jnp.int32, (size_z, size_z), 0)
    col = lax.broadcasted_iota(jnp.int32, (size_z, size_z), 1)
    along_z[...] = band(jnp.abs(row - col)).astype(jnp.bfloat16)
    row = lax.broadcasted_iota(jnp.int32, (block, block), 0)
    col = lax.broadcasted_iota(jnp.int32, (block, block), 1)
    same = lax.div(row, size_y) == lax.div(col, size_y)
    half = jnp.where(same, band(jnp.abs(row - col)), 0.0).astype(jnp.bfloat16)
    along_y[:, :block] = half
    along_y[:, block:] = half
    first = (lax.axis_index("slab") * rows - REACH) * size_y
    cells = plane_count * size_y
    lane = lax.broadcasted_iota(jnp.int32, (1, LANES), 1)
    for group in range(groups):
        ids = first + lax.broadcasted_iota(jnp.int32, (cells, 1), 0)
        amplitude = jnp.zeros((1, LANES), jnp.float32)
        for step in range(steps):
            amplitude = jnp.where(lane == step, wavelet[step, group], amplitude)
        hit = jnp.broadcast_to(ids, (cells, LANES)) == source_cell[group]
        spread = jnp.where(hit, jnp.broadcast_to(amplitude, (cells, LANES)), 0.0)
        planes[group][0] = spread.reshape(plane_count, size_y, LANES)
        count = receiver_cell.shape[1]
        wide = first + lax.broadcasted_iota(jnp.int32, (cells, count), 0)
        here = jnp.broadcast_to(receiver_cell[group : group + 1, :], (cells, count))
        hot = (wide == here).astype(jnp.float32).astype(jnp.bfloat16)
        left, terms = traces[:, group, :], []
        for _ in range(3):
            term = left.astype(jnp.bfloat16).astype(jnp.float32)
            terms.append(term)
            left = left - term
        terms.append(jnp.zeros((LANES - 3 * steps, count), jnp.float32))
        summed = lax.dot_general(
            hot,
            jnp.concatenate(terms, axis=0).astype(jnp.bfloat16),
            (((1,), (1,)), ((), ())),
            preferred_element_type=jnp.float32,
        )
        summed = summed + pltpu.roll(summed, LANES - steps, 1) + pltpu.roll(summed, LANES - 2 * steps, 1)
        planes[group][1] = summed.reshape(plane_count, size_y, LANES)
    for copy in copies:
        copy.wait()


def prepare(source_cell, wavelet, offset_perm, receiver_cell, traces, fields):
    groups, rows, size_y, size_z = fields[0].shape
    block = CHUNK * size_y
    field = struct((2, rows, size_y, size_z))
    shapes = [
        struct((size_z, size_z), jnp.bfloat16),
        struct((block, 2 * block), jnp.bfloat16),
        struct((offset_perm.shape[0], LANES), jnp.int32),
    ]
    shapes += [struct((2, rows + 2 * REACH, size_y, LANES))] * groups + [field] * (2 * groups)
    return pl.pallas_call(
        functools.partial(prepare_kernel, groups, rows),
        out_shape=shapes,
        in_specs=[smem()] * 3 + [vmem()] * 2 + [hbm()] * 4,
        out_specs=[vmem()] * len(shapes),
        scratch_shapes=[pltpu.SemaphoreType.DMA((4 * groups,))],
        compiler_params=params(),
        name="prepare",
    )(source_cell, wavelet, offset_perm, receiver_cell, traces, *stay(*fields))


def advance(now, at, before, before_at, courant, courant_at, inject, inject_at, runs, step, along_z, along_y, write):
    size_y, size_z = now.shape[-2:]
    pieces = [now[at + first : at + first + count].reshape(count * size_y, size_z) for first, count in runs]
    value = pieces[0] if len(pieces) == 1 else jnp.concatenate(pieces, axis=0)
    high = value.astype(jnp.bfloat16)
    low = (value - high.astype(jnp.float32)).astype(jnp.bfloat16)
    dot = functools.partial(jnp.dot, preferred_element_type=jnp.float32)
    sides = dot(high, along_z) + dot(low, along_z)
    sides = sides + dot(along_y, jnp.concatenate([high, low], axis=0))
    lane = lax.broadcasted_iota(jnp.int32, (size_y, LANES), 1)
    for i, plane in enumerate(first + j for first, count in runs for j in range(count)):
        here = at + plane
        own = now[here]
        total = sides[i * size_y : (i + 1) * size_y] + OWN * own
        for distance, tap in enumerate(TAPS, 1):
            pair = now[here + distance] + now[here - distance]
            total = total + (pair if tap == 1.0 else tap * pair)
        new = (own + own) - before[before_at + plane] + courant[courant_at + plane] * total
        spot = pltpu.roll(inject[inject_at + plane], (INJECT_Z - step) % LANES, 1)
        near = new[:, :LANES] + jnp.where(lane == INJECT_Z, spot, 0.0)
        write(i, plane, jnp.concatenate([near, new[:, LANES:]], axis=1))


def chunks(start, stop):
    return [[(at, CHUNK)] for at in range(start, stop, CHUNK)]


def first_kernel(rows, width, now, before, courant, even, odd, inject, along_z, along_y, fresh, held, even_edge, odd_edge, *scaled):
    even_at, odd_at = halo_starts(rows, REACH)
    if scaled:
        (courant_out,) = scaled
        courant_out[REACH : REACH + rows] = SCALE * courant[...]
        courant_out[pl.ds(even_at, REACH)] = SCALE * even[2]
        courant_out[pl.ds(odd_at, REACH)] = SCALE * odd[2]
        courant = courant_out
    z_band, y_band = along_z[...], along_y[...]
    for kind in range(2):
        field = held.at[kind]
        field[REACH : REACH + rows] = now[kind]
        field[pl.ds(even_at, REACH)] = even[kind]
        field[pl.ds(odd_at, REACH)] = odd[kind]

        def write(i, plane, new, kind=kind):
            fresh[kind, plane] = new

        for runs in chunks(0, rows):
            advance(field, REACH, before.at[kind], 0, courant, REACH, inject.at[kind], REACH, runs, 0, z_band, y_band, write)
    send(rows, width, fresh, even_edge, odd_edge)


def send(rows, width, fresh, even_edge, odd_edge):
    even_from, odd_from = edge_starts(rows, width)
    even_edge[...] = fresh[:, pl.ds(even_from, width)]
    odd_edge[...] = fresh[:, pl.ds(odd_from, width)]


def first_round(group, width, now, before, courant, halos, inject, along_z, along_y):
    rows, size_y, size_z = now.shape[1:]
    edge = struct((2, width, size_y, size_z))
    shapes = [struct(now.shape), struct((2, rows + 2 * REACH, size_y, size_z)), edge, edge]
    if group == 0:
        shapes.append(struct((rows + 2 * REACH, size_y, size_z)))
    return pl.pallas_call(
        functools.partial(first_kernel, rows, width),
        out_shape=shapes,
        in_specs=[vmem()] * 8,
        out_specs=[vmem()] * len(shapes),
        compiler_params=params(),
    )(now, before, courant, *halos, inject, along_z, along_y)


def pair_kernel(rows, step, width, now, before, even, odd, courant, inject, along_z, along_y, fresh, held, even_edge, odd_edge, wide):
    reach = 2 * REACH
    even_at, odd_at = halo_starts(rows, reach)
    z_band, y_band = along_z[...], along_y[...]
    for kind in range(2):
        field = wide.at[kind]
        field[reach : reach + rows] = now[kind]
        field[pl.ds(even_at, reach)] = even[kind]
        field[pl.ds(odd_at, reach)] = odd[kind]
        middle = held.at[kind]

        def write_middle(i, plane, new, kind=kind):
            held[kind, REACH + plane] = new

        def write(i, plane, new, kind=kind):
            fresh[kind, plane] = new

        for runs in chunks(-REACH, rows + REACH):
            advance(field, reach, before.at[kind], REACH, courant, REACH, inject.at[kind], REACH, runs, step, z_band, y_band, write_middle)
        for runs in chunks(0, rows):
            advance(middle, REACH, field, reach, courant, REACH, inject.at[kind], REACH, runs, step + 1, z_band, y_band, write)
    send(rows, width, fresh, even_edge, odd_edge)


def pair_round(step, width, now, before, halos, courant, inject, along_z, along_y):
    rows, size_y, size_z = now.shape[1:]
    edge = struct((2, width, size_y, size_z))
    shapes = [struct(now.shape), struct((2, rows + 2 * REACH, size_y, size_z)), edge, edge]
    return pl.pallas_call(
        functools.partial(pair_kernel, rows, step, width),
        out_shape=shapes,
        in_specs=[vmem()] * 8,
        out_specs=[vmem()] * 4,
        scratch_shapes=[pltpu.VMEM((2, rows + 4 * REACH, size_y, size_z), jnp.float32)],
        compiler_params=params(),
    )(now, before, *halos, courant, inject, along_z, along_y)


def inner_kernel(group, rows, step, now, before, courant, inject, along_z, along_y, *refs):
    final = refs[-1]
    z_band, y_band = along_z[...], along_y[...]
    for kind in range(2):

        def write(i, plane, new, place=2 * group + kind):
            final[place, plane - REACH] = new

        for runs in chunks(REACH, rows - REACH):
            advance(now.at[kind], 0, before.at[kind], REACH, courant, REACH, inject.at[kind], REACH, runs, step, z_band, y_band, write)


def inner_round(group, groups, step, now, before, courant, inject, along_z, along_y, final):
    rows, size_y, size_z = now.shape[1:]
    return pl.pallas_call(
        functools.partial(inner_kernel, group, rows, step),
        out_shape=struct((2 * groups, rows - 2 * REACH, size_y, size_z)),
        in_specs=[vmem()] * (6 + len(final)),
        out_specs=vmem(),
        input_output_aliases={6: 0} if final else {},
        compiler_params=params(),
    )(now, before, courant, inject, along_z, along_y, *final)


def outer_kernel(rows, step, now, before, even, odd, courant, inject, along_z, along_y, final, wide):
    even_at, odd_at = halo_starts(rows, REACH)
    z_band, y_band = along_z[...], along_y[...]
    for kind in range(2):
        field = wide.at[kind]
        field[REACH : REACH + rows] = now[kind]
        field[pl.ds(even_at, REACH)] = even[kind]
        field[pl.ds(odd_at, REACH)] = odd[kind]

        def write(i, plane, new, kind=kind):
            final[kind, i] = new

        runs = [(0, REACH), (rows - REACH, REACH)]
        advance(field, REACH, before.at[kind], REACH, courant, REACH, inject.at[kind], REACH, runs, step, z_band, y_band, write)


def outer_round(step, now, before, halos, courant, inject, along_z, along_y):
    rows, size_y, size_z = now.shape[1:]
    return pl.pallas_call(
        functools.partial(outer_kernel, rows, step),
        out_shape=struct((2, 2 * REACH, size_y, size_z)),
        in_specs=[vmem()] * 8,
        out_specs=vmem(),
        scratch_shapes=[pltpu.VMEM((2, rows + 2 * REACH, size_y, size_z), jnp.float32)],
        compiler_params=params(),
    )(now, before, *halos, courant, inject, along_z, along_y)


def shifted(plane, amount):
    size_y = plane.shape[0]
    if amount == 0:
        return plane
    if abs(amount) >= size_y:
        return jnp.zeros_like(plane)
    row = lax.broadcasted_iota(jnp.int32, plane.shape, 0)
    inside = (row >= amount) if amount > 0 else (row < size_y + amount)
    return jnp.where(inside, pltpu.roll(plane, amount % size_y, 0), 0.0)


def partial_image(ahead, lags, fields, image, others=()):
    count = lags.shape[0]
    half_span = count // 2
    slots, rows = image.shape[:2]
    here = lax.axis_index("shot")
    pairs = lax.axis_size("shot") // 2
    owner = 2 * lax.rem(lax.div(here, 2) + ahead, pairs) + lax.rem(here, 2)

    def one_slot(slot, carry):
        index = jnp.max(lags[pl.ds(owner * slots + slot, 1), :])
        for lag_index in range(count):
            lag = lag_index - half_span

            @pl.when(index == lag_index)
            def _(lag=lag):
                def one_plane(x, carry):
                    total = None
                    for field in fields:
                        for source in range(0, field.shape[0], 2):
                            term = field[source + 1, x] * shifted(field[source, x], 2 * lag)
                            total = term if total is None else total + term
                    total = shifted(total, -lag)
                    for other in others:
                        total = total + other[slot, x]
                    image[slot, x] = total
                    return carry

                lax.fori_loop(0, rows, one_plane, 0, unroll=4)

        return carry

    lax.fori_loop(0, slots, one_slot, 0)


def image_kernel(ahead, lags, *refs):
    partial_image(ahead, lags, refs[:-1], refs[-1])


def image_part(ahead, slots, lags, fields):
    _, rows, size_y, size_z = fields[0].shape
    return pl.pallas_call(
        functools.partial(image_kernel, ahead),
        out_shape=struct((slots, rows, size_y, size_z)),
        in_specs=[vmem()] * (1 + len(fields)),
        out_specs=vmem(),
        compiler_params=params(),
    )(lags, *fields)


def inner_image_kernel(groups, rows, lags, *refs):
    inner_fields, outer_fields, others = refs[:2], refs[2 : 2 + 2 * groups], refs[2 + 2 * groups : -6]
    image, source_out, receiver_out, outer, inner, sem = refs[-6:]
    copies = []
    for group in range(groups):
        for kind, out in enumerate((source_out, receiver_out)):
            pieces = (
                (inner_fields[0].at[2 * group + kind], REACH, rows - 2 * REACH),
                (outer_fields[group].at[kind, pl.ds(0, REACH)], 0, REACH),
                (outer_fields[group].at[kind, pl.ds(REACH, REACH)], rows - REACH, REACH),
            )
            for piece, first, count in pieces:
                copies.append(pltpu.make_async_copy(piece, out.at[group, pl.ds(first, count)], sem.at[len(copies)]))
                copies[-1].start()
    partial_image(0, lags, inner_fields, inner, others)
    copies.append(pltpu.make_async_copy(inner, image.at[:, pl.ds(REACH, rows - 2 * REACH)], sem.at[len(copies)]))
    copies[-1].start()
    partial_image(0, lags, outer_fields, outer)
    for copy in copies:
        copy.wait()


def inner_image(slots, inner, outer, others, lags):
    places, inner_rows, size_y, size_z = inner[0].shape
    groups, rows = places // 2, inner_rows + 2 * REACH
    whole = struct((groups, rows, size_y, size_z))
    return pl.pallas_call(
        functools.partial(inner_image_kernel, groups, rows),
        out_shape=[struct((slots, rows, size_y, size_z)), whole, whole, struct((slots, 2 * REACH, size_y, size_z))],
        in_specs=[vmem()] * (1 + len(inner) + len(outer) + len(others)),
        out_specs=[hbm()] * 3 + [vmem()],
        scratch_shapes=[pltpu.VMEM((slots, inner_rows, size_y, size_z), jnp.float32), pltpu.SemaphoreType.DMA((3 * places + 1,))],
        compiler_params=params(),
        name="image_inner",
    )(lags, *inner, *outer, *others)


def outer_image_kernel(rows, *refs):
    own, others = refs[0], refs[1:-4]
    image, outer, sem = refs[-3:]
    copies = []
    for side, first in enumerate((0, rows - REACH)):
        planes = pl.ds(side * REACH, REACH)
        total = own[:, planes]
        for other in others:
            total = total + other[:, planes]
        outer[:, planes] = total
        copies.append(pltpu.make_async_copy(outer.at[:, planes], image.at[:, pl.ds(first, REACH)], sem.at[side]))
        copies[side].start()
    for copy in copies:
        copy.wait()


def outer_image(image, own, others):
    return pl.pallas_call(
        functools.partial(outer_image_kernel, image.shape[1]),
        out_shape=struct(image.shape),
        in_specs=[vmem()] * (1 + len(others)) + [hbm()],
        out_specs=hbm(),
        scratch_shapes=[pltpu.VMEM(own.shape, jnp.float32), pltpu.SemaphoreType.DMA((2,))],
        input_output_aliases={1 + len(others): 0},
        compiler_params=params(),
        name="image_outer",
    )(own, *others, image)


def program(source_now, source_prev, receiver_now, receiver_prev, courant_sq, source_cell, wavelet, receiver_cell, traces, offset_perm):
    groups, _, _, _ = source_now.shape
    steps = wavelet.shape[0]
    shot_devices = lax.axis_size("shot")
    slots = offset_perm.shape[0] // shot_devices
    everyone = range(groups)

    edges = pack(source_now, receiver_now, courant_sq)
    given = [trade(edges[2 * g], edges[2 * g + 1]) for g in everyone]
    fields = (source_now, receiver_now, source_prev, receiver_prev)
    along_z, along_y, lags, *rest = prepare(source_cell, wavelet, offset_perm, receiver_cell, traces, fields)
    inject, now, before = rest[:groups], rest[groups : 2 * groups], rest[2 * groups :]

    halos = [None] * groups
    courant = courant_sq
    for g in everyone:
        result = first_round(g, 2 * REACH, now[g], before[g], courant, given[g], inject[g], along_z, along_y)
        now[g], before[g] = result[:2]
        if g == 0:
            courant = result[4]
        halos[g] = trade(*result[2:4])
    final = ()
    for step in range(1, steps - 1, 2):
        last = step + 2 >= steps - 1
        for g in everyone:
            now[g], before[g], even, odd = pair_round(step, REACH if last else 2 * REACH, now[g], before[g], halos[g], courant, inject[g], along_z, along_y)
            halos[g] = trade(even, odd)
            if last:
                final = (inner_round(g, groups, steps - 1, now[g], before[g], courant, inject[g], along_z, along_y, final),)

    swap = [(i, i ^ 1) for i in range(shot_devices)]
    pairs = shot_devices // 2

    def traded(own):
        return lax.ppermute(own, "shot", swap)

    def part_sums(fields):
        parts = [image_part(ahead, slots, lags, fields) for ahead in range(1, pairs)]
        sums = []
        for ahead, part in enumerate(parts, 1):
            route = [(2 * p + c, 2 * ((p + ahead) % pairs) + c) for p in range(pairs) for c in range(2)]
            sums.append(lax.ppermute(part, "shot", route))
        return sums

    inner = (*final, traded(*final))
    inner_sums = part_sums(inner)
    own, other = [], []
    for g in everyone:
        own.append(outer_round(steps - 1, now[g], before[g], halos[g], courant, inject[g], along_z, along_y))
        other.append(traded(own[g]))
    outer = (*own, *other)
    outer_sums = part_sums(outer)
    image, source_final, receiver_final, part = inner_image(slots, inner, outer, inner_sums, lags)
    image = outer_image(image, part, outer_sums)
    return image, source_final, receiver_final


def solution(mesh):
    shots = ("runs", "shot")
    in_specs = (
        P(shots, "slab", None, None),
        P(shots, "slab", None, None),
        P(shots, "slab", None, None),
        P(shots, "slab", None, None),
        P(("runs", "slab"), None, None),
        P(shots),
        P(None, shots),
        P(shots, None),
        P(None, shots, None),
        P("runs"),
    )
    out_specs = (P(shots, "slab", None, None),) * 3
    return jax.shard_map(program, mesh=mesh, in_specs=in_specs, out_specs=out_specs, check_vma=False)
```

```python
import functools

import jax
import jax.numpy as jnp
from jax import lax
from jax.experimental import pallas as pl
from jax.experimental.pallas import tpu as pltpu
from jax.sharding import PartitionSpec as P


REACH = 4
INJECT_Z = 4
LANES = 128
CHUNK = 8

SCALE = 8.0 / 5.0
SIDE = 1.0 / 16.0
OWN = (1.0 + 2.0 * SIDE) * (-205.0 / 72.0) / SCALE
TAPS = (1.0, -1.0 / 8.0, 1.0 / 63.0, -1.0 / 896.0)

VMEM_LIMIT = 24 * 1024 * 1024


def vmem():
    return pl.BlockSpec(memory_space=pltpu.VMEM)


def smem():
    return pl.BlockSpec(memory_space=pltpu.SMEM)


def hbm():
    return pl.BlockSpec(memory_space=pltpu.HBM)


def params():
    return pltpu.CompilerParams(vmem_limit_bytes=VMEM_LIMIT)


def struct(shape, dtype=jnp.float32):
    return jax.ShapeDtypeStruct(shape, dtype)


def even_pairs(count):
    pairs = []
    for i in range(0, count - 1, 2):
        pairs += [(i, i + 1), (i + 1, i)]
    return pairs


def odd_pairs(count):
    pairs = []
    for i in range(1, count - 1, 2):
        pairs += [(i, i + 1), (i + 1, i)]
    return pairs


def trade(even_edge, odd_edge):
    count = lax.axis_size("slab")
    even = lax.ppermute(even_edge, "slab", even_pairs(count))
    odd = lax.ppermute(odd_edge, "slab", odd_pairs(count))
    return even, odd


def parity():
    return lax.rem(lax.axis_index("slab"), 2)


def edge_starts(rows, width):
    odd = parity()
    return (1 - odd) * (rows - width), odd * (rows - width)


def halo_starts(rows, width):
    odd = parity()
    return (1 - odd) * (rows + width), odd * (rows + width)


def pack_kernel(source, receiver, courant, *refs):
    groups, rows = source.shape[:2]
    outs, sem = refs[:-1], refs[-1]
    copies = []
    for group in range(groups):
        for side, start in enumerate(edge_starts(rows, REACH)):
            planes = pl.ds(start, REACH)
            pieces = [source.at[group, planes], receiver.at[group, planes]]
            if group == groups - 1:
                pieces.append(courant.at[planes])
            for index, piece in enumerate(pieces):
                copies.append(pltpu.make_async_copy(piece, outs[2 * group + side].at[index], sem.at[len(copies)]))
    for copy in copies:
        copy.start()
    for copy in copies:
        copy.wait()


def stay(*arrays):
    return [pltpu.with_memory_space_constraint(array, pltpu.HBM) for array in arrays]


def pack(source_now, receiver_now, courant_sq):
    groups, _, size_y, size_z = source_now.shape
    shapes = [struct((3 if group == groups - 1 else 2, REACH, size_y, size_z)) for group in range(groups) for _ in range(2)]
    return pl.pallas_call(
        pack_kernel,
        out_shape=shapes,
        in_specs=[hbm()] * 3,
        out_specs=[vmem()] * len(shapes),
        scratch_shapes=[pltpu.SemaphoreType.DMA((4 * groups + 2,))],
        compiler_params=params(),
        name="pack",
    )(*stay(source_now, receiver_now, courant_sq))


def band(distance):
    value = jnp.zeros(distance.shape, jnp.float32)
    for step, tap in enumerate(TAPS):
        value = jnp.where(distance == step + 1, SIDE * tap, value)
    return value


def fetch(pieces, sem):
    copies = [pltpu.make_async_copy(array, place, sem.at[index]) for index, (array, place) in enumerate(pieces)]
    for copy in copies:
        copy.start()
    return copies


def prepare_kernel(group, rows, source_cell, wavelet, offset_perm, receiver_cell, traces, source, receiver, source_before, receiver_before, planes, now, before, *refs):
    tables, sem = refs[:-1], refs[-1]
    pieces = [(source.at[group], now.at[0]), (receiver.at[group], now.at[1])]
    pieces += [(source_before.at[group], before.at[0]), (receiver_before.at[group], before.at[1])]
    copies = fetch(pieces, sem)
    if tables:
        make_tables(planes.shape[2], offset_perm, *tables)
    spread_data(group, rows, source_cell, wavelet, receiver_cell, traces, planes)
    for copy in copies:
        copy.wait()


def make_tables(size_y, offset_perm, along_z, along_y, lags):
    size_z = along_z.shape[0]
    block = along_y.shape[0]
    for slot in range(offset_perm.shape[0]):
        lags[slot : slot + 1, :] = jnp.full((1, LANES), offset_perm[slot], jnp.int32)
    row = lax.broadcasted_iota(jnp.int32, (size_z, size_z), 0)
    col = lax.broadcasted_iota(jnp.int32, (size_z, size_z), 1)
    along_z[...] = band(jnp.abs(row - col)).astype(jnp.bfloat16)
    row = lax.broadcasted_iota(jnp.int32, (block, block), 0)
    col = lax.broadcasted_iota(jnp.int32, (block, block), 1)
    same = lax.div(row, size_y) == lax.div(col, size_y)
    half = jnp.where(same, band(jnp.abs(row - col)), 0.0).astype(jnp.bfloat16)
    along_y[:, :block] = half
    along_y[:, block:] = half


def spread_data(group, rows, source_cell, wavelet, receiver_cell, traces, planes):
    _, plane_count, size_y, _ = planes.shape
    steps = traces.shape[0]
    first = (lax.axis_index("slab") * rows - REACH) * size_y
    cells = plane_count * size_y
    lane = lax.broadcasted_iota(jnp.int32, (1, LANES), 1)
    ids = first + lax.broadcasted_iota(jnp.int32, (cells, 1), 0)
    amplitude = jnp.zeros((1, LANES), jnp.float32)
    for step in range(steps):
        amplitude = jnp.where(lane == step, wavelet[step, group], amplitude)
    hit = jnp.broadcast_to(ids, (cells, LANES)) == source_cell[group]
    spread = jnp.where(hit, jnp.broadcast_to(amplitude, (cells, LANES)), 0.0)
    planes[0] = spread.reshape(plane_count, size_y, LANES)
    count = receiver_cell.shape[1]
    wide = first + lax.broadcasted_iota(jnp.int32, (cells, count), 0)
    here = jnp.broadcast_to(receiver_cell[group : group + 1, :], (cells, count))
    hot = (wide == here).astype(jnp.float32).astype(jnp.bfloat16)
    left, terms = traces[:, group, :], []
    for _ in range(3):
        term = left.astype(jnp.bfloat16).astype(jnp.float32)
        terms.append(term)
        left = left - term
    terms.append(jnp.zeros((LANES - 3 * steps, count), jnp.float32))
    summed = lax.dot_general(
        hot,
        jnp.concatenate(terms, axis=0).astype(jnp.bfloat16),
        (((1,), (1,)), ((), ())),
        preferred_element_type=jnp.float32,
    )
    summed = summed + pltpu.roll(summed, LANES - steps, 1) + pltpu.roll(summed, LANES - 2 * steps, 1)
    planes[1] = summed.reshape(plane_count, size_y, LANES)


def prepare(group, source_cell, wavelet, offset_perm, receiver_cell, traces, fields):
    _, rows, size_y, size_z = fields[0].shape
    block = CHUNK * size_y
    field = struct((2, rows, size_y, size_z))
    shapes = [struct((2, rows + 2 * REACH, size_y, LANES)), field, field]
    if group == 0:
        shapes += [
            struct((size_z, size_z), jnp.bfloat16),
            struct((block, 2 * block), jnp.bfloat16),
            struct((offset_perm.shape[0], LANES), jnp.int32),
        ]
    return pl.pallas_call(
        functools.partial(prepare_kernel, group, rows),
        out_shape=shapes,
        in_specs=[smem()] * 3 + [vmem()] * 2 + [hbm()] * 4,
        out_specs=[vmem()] * len(shapes),
        scratch_shapes=[pltpu.SemaphoreType.DMA((4,))],
        compiler_params=params(),
    )(source_cell, wavelet, offset_perm, receiver_cell, traces, *stay(*fields))


def advance(now, at, before, before_at, courant, courant_at, inject, inject_at, runs, step, along_z, along_y, write):
    size_y, size_z = now.shape[-2:]
    pieces = [now[at + first : at + first + count].reshape(count * size_y, size_z) for first, count in runs]
    value = pieces[0] if len(pieces) == 1 else jnp.concatenate(pieces, axis=0)
    high = value.astype(jnp.bfloat16)
    low = (value - high.astype(jnp.float32)).astype(jnp.bfloat16)
    dot = functools.partial(jnp.dot, preferred_element_type=jnp.float32)
    sides = dot(high, along_z) + dot(low, along_z)
    sides = sides + dot(along_y, jnp.concatenate([high, low], axis=0))
    lane = lax.broadcasted_iota(jnp.int32, (size_y, LANES), 1)
    for i, plane in enumerate(first + j for first, count in runs for j in range(count)):
        here = at + plane
        own = now[here]
        total = sides[i * size_y : (i + 1) * size_y] + OWN * own
        for distance, tap in enumerate(TAPS, 1):
            pair = now[here + distance] + now[here - distance]
            total = total + (pair if tap == 1.0 else tap * pair)
        new = (own + own) - before[before_at + plane] + courant[courant_at + plane] * total
        spot = pltpu.roll(inject[inject_at + plane], (INJECT_Z - step) % LANES, 1)
        near = new[:, :LANES] + jnp.where(lane == INJECT_Z, spot, 0.0)
        write(i, plane, jnp.concatenate([near, new[:, LANES:]], axis=1))


def chunks(start, stop):
    return [[(at, CHUNK)] for at in range(start, stop, CHUNK)]


def first_kernel(rows, last, width, now, before, courant, even, odd, inject, along_z, along_y, fresh, held, even_edge, odd_edge, scaled):
    even_at, odd_at = halo_starts(rows, REACH)
    inside = REACH if last else 0
    scaled[inside : inside + rows] = SCALE * courant[...]
    if last:
        scaled[pl.ds(even_at, REACH)] = SCALE * even[2]
        scaled[pl.ds(odd_at, REACH)] = SCALE * odd[2]
    z_band, y_band = along_z[...], along_y[...]
    for kind in range(2):
        field = held.at[kind]
        field[REACH : REACH + rows] = now[kind]
        field[pl.ds(even_at, REACH)] = even[kind]
        field[pl.ds(odd_at, REACH)] = odd[kind]

        def write(i, plane, new, kind=kind):
            fresh[kind, plane] = new

        for runs in chunks(0, rows):
            advance(field, REACH, before.at[kind], 0, scaled, inside, inject.at[kind], REACH, runs, 0, z_band, y_band, write)
    send(rows, width, fresh, even_edge, odd_edge)


def send(rows, width, fresh, even_edge, odd_edge):
    even_from, odd_from = edge_starts(rows, width)
    even_edge[...] = fresh[:, pl.ds(even_from, width)]
    odd_edge[...] = fresh[:, pl.ds(odd_from, width)]


def first_round(group, groups, width, now, before, courant, halos, inject, along_z, along_y):
    rows, size_y, size_z = now.shape[1:]
    last = group == groups - 1
    edge = struct((2, width, size_y, size_z))
    shapes = [struct(now.shape), struct((2, rows + 2 * REACH, size_y, size_z)), edge, edge]
    scratch = []
    if last:
        shapes.append(struct((rows + 2 * REACH, size_y, size_z)))
    else:
        scratch.append(pltpu.VMEM((rows, size_y, size_z), jnp.float32))
    return pl.pallas_call(
        functools.partial(first_kernel, rows, last, width),
        out_shape=shapes,
        in_specs=[vmem()] * 8,
        out_specs=[vmem()] * len(shapes),
        scratch_shapes=scratch,
        compiler_params=params(),
    )(now, before, courant, *halos, inject, along_z, along_y)


def pair_kernel(rows, step, width, now, before, even, odd, courant, inject, along_z, along_y, fresh, held, even_edge, odd_edge, wide):
    reach = 2 * REACH
    even_at, odd_at = halo_starts(rows, reach)
    z_band, y_band = along_z[...], along_y[...]
    for kind in range(2):
        field = wide.at[kind]
        field[reach : reach + rows] = now[kind]
        field[pl.ds(even_at, reach)] = even[kind]
        field[pl.ds(odd_at, reach)] = odd[kind]
        middle = held.at[kind]

        def write_middle(i, plane, new, kind=kind):
            held[kind, REACH + plane] = new

        def write(i, plane, new, kind=kind):
            fresh[kind, plane] = new

        for runs in chunks(-REACH, rows + REACH):
            advance(field, reach, before.at[kind], REACH, courant, REACH, inject.at[kind], REACH, runs, step, z_band, y_band, write_middle)
        for runs in chunks(0, rows):
            advance(middle, REACH, field, reach, courant, REACH, inject.at[kind], REACH, runs, step + 1, z_band, y_band, write)
    send(rows, width, fresh, even_edge, odd_edge)


def pair_round(step, width, now, before, halos, courant, inject, along_z, along_y):
    rows, size_y, size_z = now.shape[1:]
    edge = struct((2, width, size_y, size_z))
    shapes = [struct(now.shape), struct((2, rows + 2 * REACH, size_y, size_z)), edge, edge]
    return pl.pallas_call(
        functools.partial(pair_kernel, rows, step, width),
        out_shape=shapes,
        in_specs=[vmem()] * 8,
        out_specs=[vmem()] * 4,
        scratch_shapes=[pltpu.VMEM((2, rows + 4 * REACH, size_y, size_z), jnp.float32)],
        compiler_params=params(),
    )(now, before, *halos, courant, inject, along_z, along_y)


def inner_kernel(group, rows, step, now, before, courant, inject, along_z, along_y, *refs):
    final = refs[-1]
    z_band, y_band = along_z[...], along_y[...]
    for kind in range(2):

        def write(i, plane, new, place=2 * group + kind):
            final[place, plane - REACH] = new

        for runs in chunks(REACH, rows - REACH):
            advance(now.at[kind], 0, before.at[kind], REACH, courant, REACH, inject.at[kind], REACH, runs, step, z_band, y_band, write)


def inner_round(group, groups, step, now, before, courant, inject, along_z, along_y, final):
    rows, size_y, size_z = now.shape[1:]
    return pl.pallas_call(
        functools.partial(inner_kernel, group, rows, step),
        out_shape=struct((2 * groups, rows - 2 * REACH, size_y, size_z)),
        in_specs=[vmem()] * (6 + len(final)),
        out_specs=vmem(),
        input_output_aliases={6: 0} if final else {},
        compiler_params=params(),
    )(now, before, courant, inject, along_z, along_y, *final)


def outer_kernel(rows, step, now, before, even, odd, courant, inject, along_z, along_y, final, wide):
    even_at, odd_at = halo_starts(rows, REACH)
    z_band, y_band = along_z[...], along_y[...]
    for kind in range(2):
        field = wide.at[kind]
        field[REACH : REACH + rows] = now[kind]
        field[pl.ds(even_at, REACH)] = even[kind]
        field[pl.ds(odd_at, REACH)] = odd[kind]

        def write(i, plane, new, kind=kind):
            final[kind, i] = new

        runs = [(0, REACH), (rows - REACH, REACH)]
        advance(field, REACH, before.at[kind], REACH, courant, REACH, inject.at[kind], REACH, runs, step, z_band, y_band, write)


def outer_round(step, now, before, halos, courant, inject, along_z, along_y):
    rows, size_y, size_z = now.shape[1:]
    return pl.pallas_call(
        functools.partial(outer_kernel, rows, step),
        out_shape=struct((2, 2 * REACH, size_y, size_z)),
        in_specs=[vmem()] * 8,
        out_specs=vmem(),
        scratch_shapes=[pltpu.VMEM((2, rows + 2 * REACH, size_y, size_z), jnp.float32)],
        compiler_params=params(),
    )(now, before, *halos, courant, inject, along_z, along_y)


def shifted(plane, amount):
    size_y = plane.shape[0]
    if amount == 0:
        return plane
    if abs(amount) >= size_y:
        return jnp.zeros_like(plane)
    row = lax.broadcasted_iota(jnp.int32, plane.shape, 0)
    inside = (row >= amount) if amount > 0 else (row < size_y + amount)
    return jnp.where(inside, pltpu.roll(plane, amount % size_y, 0), 0.0)


def partial_image(ahead, lags, fields, image, others=()):
    count = lags.shape[0]
    half_span = count // 2
    slots, rows = image.shape[:2]
    here = lax.axis_index("shot")
    pairs = lax.axis_size("shot") // 2
    owner = 2 * lax.rem(lax.div(here, 2) + ahead, pairs) + lax.rem(here, 2)

    def one_slot(slot, carry):
        index = jnp.max(lags[pl.ds(owner * slots + slot, 1), :])
        for lag_index in range(count):
            lag = lag_index - half_span

            @pl.when(index == lag_index)
            def _(lag=lag):
                def one_plane(x, carry):
                    total = None
                    for field in fields:
                        for source in range(0, field.shape[0], 2):
                            term = field[source + 1, x] * shifted(field[source, x], 2 * lag)
                            total = term if total is None else total + term
                    total = shifted(total, -lag)
                    for other in others:
                        total = total + other[slot, x]
                    image[slot, x] = total
                    return carry

                lax.fori_loop(0, rows, one_plane, 0, unroll=4)

        return carry

    lax.fori_loop(0, slots, one_slot, 0)


def image_kernel(ahead, lags, *refs):
    partial_image(ahead, lags, refs[:-1], refs[-1])


def image_part(ahead, slots, lags, fields):
    _, rows, size_y, size_z = fields[0].shape
    return pl.pallas_call(
        functools.partial(image_kernel, ahead),
        out_shape=struct((slots, rows, size_y, size_z)),
        in_specs=[vmem()] * (1 + len(fields)),
        out_specs=vmem(),
        compiler_params=params(),
    )(lags, *fields)


def inner_image_kernel(groups, rows, lags, *refs):
    inner_fields, outer_fields, others = refs[:2], refs[2 : 2 + 2 * groups], refs[2 + 2 * groups : -6]
    image, source_out, receiver_out, outer, inner, sem = refs[-6:]
    copies = []
    for group in range(groups):
        for kind, out in enumerate((source_out, receiver_out)):
            pieces = (
                (inner_fields[0].at[2 * group + kind], REACH, rows - 2 * REACH),
                (outer_fields[group].at[kind, pl.ds(0, REACH)], 0, REACH),
                (outer_fields[group].at[kind, pl.ds(REACH, REACH)], rows - REACH, REACH),
            )
            for piece, first, count in pieces:
                copies.append(pltpu.make_async_copy(piece, out.at[group, pl.ds(first, count)], sem.at[len(copies)]))
                copies[-1].start()
    partial_image(0, lags, inner_fields, inner, others)
    copies.append(pltpu.make_async_copy(inner, image.at[:, pl.ds(REACH, rows - 2 * REACH)], sem.at[len(copies)]))
    copies[-1].start()
    partial_image(0, lags, outer_fields, outer)
    for copy in copies:
        copy.wait()


def inner_image(slots, inner, outer, others, lags):
    places, inner_rows, size_y, size_z = inner[0].shape
    groups, rows = places // 2, inner_rows + 2 * REACH
    whole = struct((groups, rows, size_y, size_z))
    return pl.pallas_call(
        functools.partial(inner_image_kernel, groups, rows),
        out_shape=[struct((slots, rows, size_y, size_z)), whole, whole, struct((slots, 2 * REACH, size_y, size_z))],
        in_specs=[vmem()] * (1 + len(inner) + len(outer) + len(others)),
        out_specs=[hbm()] * 3 + [vmem()],
        scratch_shapes=[pltpu.VMEM((slots, inner_rows, size_y, size_z), jnp.float32), pltpu.SemaphoreType.DMA((3 * places + 1,))],
        compiler_params=params(),
        name="image_inner",
    )(lags, *inner, *outer, *others)


def outer_image_kernel(rows, *refs):
    own, others = refs[0], refs[1:-4]
    image, outer, sem = refs[-3:]
    copies = []
    for side, first in enumerate((0, rows - REACH)):
        planes = pl.ds(side * REACH, REACH)
        total = own[:, planes]
        for other in others:
            total = total + other[:, planes]
        outer[:, planes] = total
        copies.append(pltpu.make_async_copy(outer.at[:, planes], image.at[:, pl.ds(first, REACH)], sem.at[side]))
        copies[side].start()
    for copy in copies:
        copy.wait()


def outer_image(image, own, others):
    return pl.pallas_call(
        functools.partial(outer_image_kernel, image.shape[1]),
        out_shape=struct(image.shape),
        in_specs=[vmem()] * (1 + len(others)) + [hbm()],
        out_specs=hbm(),
        scratch_shapes=[pltpu.VMEM(own.shape, jnp.float32), pltpu.SemaphoreType.DMA((2,))],
        input_output_aliases={1 + len(others): 0},
        compiler_params=params(),
        name="image_outer",
    )(own, *others, image)


def program(source_now, source_prev, receiver_now, receiver_prev, courant_sq, source_cell, wavelet, receiver_cell, traces, offset_perm):
    groups, _, _, _ = source_now.shape
    steps = wavelet.shape[0]
    shot_devices = lax.axis_size("shot")
    slots = offset_perm.shape[0] // shot_devices
    everyone = range(groups)

    edges = pack(source_now, receiver_now, courant_sq)
    given = [trade(edges[2 * g], edges[2 * g + 1]) for g in everyone]
    fields = (source_now, receiver_now, source_prev, receiver_prev)
    inject, now, before = [None] * groups, [None] * groups, [None] * groups
    for g in everyone:
        inject[g], now[g], before[g], *tables = prepare(g, source_cell, wavelet, offset_perm, receiver_cell, traces, fields)
        if g == 0:
            along_z, along_y, lags = tables

    halos = [None] * groups
    for g in everyone:
        result = first_round(g, groups, 2 * REACH, now[g], before[g], courant_sq, given[g], inject[g], along_z, along_y)
        now[g], before[g] = result[:2]
        halos[g] = trade(*result[2:4])
    courant = result[4]
    final = ()
    for step in range(1, steps - 1, 2):
        last = step + 2 >= steps - 1
        for g in everyone:
            now[g], before[g], even, odd = pair_round(step, REACH if last else 2 * REACH, now[g], before[g], halos[g], courant, inject[g], along_z, along_y)
            halos[g] = trade(even, odd)
            if last:
                final = (inner_round(g, groups, steps - 1, now[g], before[g], courant, inject[g], along_z, along_y, final),)

    swap = [(i, i ^ 1) for i in range(shot_devices)]
    pairs = shot_devices // 2

    def traded(own):
        return lax.ppermute(own, "shot", swap)

    def part_sums(fields):
        parts = [image_part(ahead, slots, lags, fields) for ahead in range(1, pairs)]
        sums = []
        for ahead, part in enumerate(parts, 1):
            route = [(2 * p + c, 2 * ((p + ahead) % pairs) + c) for p in range(pairs) for c in range(2)]
            sums.append(lax.ppermute(part, "shot", route))
        return sums

    inner = (*final, traded(*final))
    inner_sums = part_sums(inner)
    own, other = [], []
    for g in everyone:
        own.append(outer_round(steps - 1, now[g], before[g], halos[g], courant, inject[g], along_z, along_y))
        other.append(traded(own[g]))
    outer = (*own, *other)
    outer_sums = part_sums(outer)
    image, source_final, receiver_final, part = inner_image(slots, inner, outer, inner_sums, lags)
    image = outer_image(image, part, outer_sums)
    return image, source_final, receiver_final


def solution(mesh):
    shots = ("runs", "shot")
    in_specs = (
        P(shots, "slab", None, None),
        P(shots, "slab", None, None),
        P(shots, "slab", None, None),
        P(shots, "slab", None, None),
        P(("runs", "slab"), None, None),
        P(shots),
        P(None, shots),
        P(shots, None),
        P(None, shots, None),
        P("runs"),
    )
    out_specs = (P(shots, "slab", None, None),) * 3
    return jax.shard_map(program, mesh=mesh, in_specs=in_specs, out_specs=out_specs, check_vma=False)
```

```python
import functools

import jax
import jax.numpy as jnp
from jax import lax
from jax.experimental import pallas as pl
from jax.experimental.pallas import tpu as pltpu
from jax.sharding import PartitionSpec as P


REACH = 4
INJECT_Z = 4
LANES = 128
CHUNK = 8

SCALE = 8.0 / 5.0
SIDE = 1.0 / 16.0
OWN = (1.0 + 2.0 * SIDE) * (-205.0 / 72.0) / SCALE
TAPS = (1.0, -1.0 / 8.0, 1.0 / 63.0, -1.0 / 896.0)

VMEM_LIMIT = 24 * 1024 * 1024


def vmem():
    return pl.BlockSpec(memory_space=pltpu.VMEM)


def smem():
    return pl.BlockSpec(memory_space=pltpu.SMEM)


def hbm():
    return pl.BlockSpec(memory_space=pltpu.HBM)


def params():
    return pltpu.CompilerParams(vmem_limit_bytes=VMEM_LIMIT)


def struct(shape, dtype=jnp.float32):
    return jax.ShapeDtypeStruct(shape, dtype)


def even_pairs(count):
    pairs = []
    for i in range(0, count - 1, 2):
        pairs += [(i, i + 1), (i + 1, i)]
    return pairs


def odd_pairs(count):
    pairs = []
    for i in range(1, count - 1, 2):
        pairs += [(i, i + 1), (i + 1, i)]
    return pairs


def trade(even_edge, odd_edge):
    count = lax.axis_size("slab")
    even = lax.ppermute(even_edge, "slab", even_pairs(count))
    odd = lax.ppermute(odd_edge, "slab", odd_pairs(count))
    return even, odd


def parity():
    return lax.rem(lax.axis_index("slab"), 2)


def edge_starts(rows, width):
    odd = parity()
    return (1 - odd) * (rows - width), odd * (rows - width)


def halo_starts(rows, width):
    odd = parity()
    return (1 - odd) * (rows + width), odd * (rows + width)


def pack_kernel(source, receiver, courant, *refs):
    groups, rows = source.shape[:2]
    outs, sem = refs[:-1], refs[-1]
    copies = []
    for group in range(groups):
        for side, start in enumerate(edge_starts(rows, REACH)):
            planes = pl.ds(start, REACH)
            pieces = [source.at[group, planes], receiver.at[group, planes]]
            if group == groups - 1:
                pieces.append(courant.at[planes])
            for index, piece in enumerate(pieces):
                copies.append(pltpu.make_async_copy(piece, outs[2 * group + side].at[index], sem.at[len(copies)]))
    for copy in copies:
        copy.start()
    for copy in copies:
        copy.wait()


def stay(*arrays):
    return [pltpu.with_memory_space_constraint(array, pltpu.HBM) for array in arrays]


def pack(source_now, receiver_now, courant_sq):
    groups, _, size_y, size_z = source_now.shape
    shapes = [struct((3 if group == groups - 1 else 2, REACH, size_y, size_z)) for group in range(groups) for _ in range(2)]
    return pl.pallas_call(
        pack_kernel,
        out_shape=shapes,
        in_specs=[hbm()] * 3,
        out_specs=[vmem()] * len(shapes),
        scratch_shapes=[pltpu.SemaphoreType.DMA((4 * groups + 2,))],
        compiler_params=params(),
        name="pack",
    )(*stay(source_now, receiver_now, courant_sq))


def band(distance):
    value = jnp.zeros(distance.shape, jnp.float32)
    for step, tap in enumerate(TAPS):
        value = jnp.where(distance == step + 1, SIDE * tap, value)
    return value


def fetch(pieces, sem):
    copies = [pltpu.make_async_copy(array, place, sem.at[index]) for index, (array, place) in enumerate(pieces)]
    for copy in copies:
        copy.start()
    return copies


def prepare_kernel(group, rows, count, source_cell, wavelet, *refs):
    prepare_shot(group, rows, refs[:count], source_cell, wavelet, *refs[count:])


def prepare_shot(group, rows, offsets, source_cell, wavelet, receiver_cell, traces, source, receiver, source_before, receiver_before, planes, now, before, *refs):
    tables, sem = refs[:-1], refs[-1]
    pieces = [(source.at[group], now.at[0]), (receiver.at[group], now.at[1])]
    pieces += [(source_before.at[group], before.at[0]), (receiver_before.at[group], before.at[1])]
    copies = fetch(pieces, sem)
    if offsets:
        (offset_perm,), lags = offsets, tables[-1]
        for slot in range(offset_perm.shape[0]):
            lags[slot : slot + 1, :] = jnp.full((1, LANES), offset_perm[slot], jnp.int32)
    if group == 0:
        make_bands(planes.shape[2], *tables[:2])
    spread_data(group, rows, source_cell, wavelet, receiver_cell, traces, planes)
    for copy in copies:
        copy.wait()


def make_bands(size_y, along_z, along_y):
    size_z = along_z.shape[0]
    block = along_y.shape[0]
    row = lax.broadcasted_iota(jnp.int32, (size_z, size_z), 0)
    col = lax.broadcasted_iota(jnp.int32, (size_z, size_z), 1)
    along_z[...] = band(jnp.abs(row - col)).astype(jnp.bfloat16)
    row = lax.broadcasted_iota(jnp.int32, (block, block), 0)
    col = lax.broadcasted_iota(jnp.int32, (block, block), 1)
    same = lax.div(row, size_y) == lax.div(col, size_y)
    half = jnp.where(same, band(jnp.abs(row - col)), 0.0).astype(jnp.bfloat16)
    along_y[:, :block] = half
    along_y[:, block:] = half


def spread_data(group, rows, source_cell, wavelet, receiver_cell, traces, planes):
    _, plane_count, size_y, _ = planes.shape
    steps = traces.shape[0]
    first = (lax.axis_index("slab") * rows - REACH) * size_y
    cells = plane_count * size_y
    lane = lax.broadcasted_iota(jnp.int32, (1, LANES), 1)
    ids = first + lax.broadcasted_iota(jnp.int32, (cells, 1), 0)
    amplitude = jnp.zeros((1, LANES), jnp.float32)
    for step in range(steps):
        amplitude = jnp.where(lane == step, wavelet[step, group], amplitude)
    hit = jnp.broadcast_to(ids, (cells, LANES)) == source_cell[group]
    spread = jnp.where(hit, jnp.broadcast_to(amplitude, (cells, LANES)), 0.0)
    planes[0] = spread.reshape(plane_count, size_y, LANES)
    count = receiver_cell.shape[1]
    wide = first + lax.broadcasted_iota(jnp.int32, (cells, count), 0)
    here = jnp.broadcast_to(receiver_cell[group : group + 1, :], (cells, count))
    hot = (wide == here).astype(jnp.float32).astype(jnp.bfloat16)
    left, terms = traces[:, group, :], []
    for _ in range(3):
        term = left.astype(jnp.bfloat16).astype(jnp.float32)
        terms.append(term)
        left = left - term
    terms.append(jnp.zeros((LANES - 3 * steps, count), jnp.float32))
    summed = lax.dot_general(
        hot,
        jnp.concatenate(terms, axis=0).astype(jnp.bfloat16),
        (((1,), (1,)), ((), ())),
        preferred_element_type=jnp.float32,
    )
    summed = summed + pltpu.roll(summed, LANES - steps, 1) + pltpu.roll(summed, LANES - 2 * steps, 1)
    planes[1] = summed.reshape(plane_count, size_y, LANES)


def prepare(group, source_cell, wavelet, offset_perm, receiver_cell, traces, fields):
    _, rows, size_y, size_z = fields[0].shape
    block = CHUNK * size_y
    field = struct((2, rows, size_y, size_z))
    shapes = [struct((2, rows + 2 * REACH, size_y, LANES)), field, field]
    if group == 0:
        shapes += [
            struct((size_z, size_z), jnp.bfloat16),
            struct((block, 2 * block), jnp.bfloat16),
        ]
    offsets = (offset_perm,) if group == source_cell.shape[0] - 1 else ()
    if offsets:
        shapes.append(struct((offset_perm.shape[0], LANES), jnp.int32))
    return pl.pallas_call(
        functools.partial(prepare_kernel, group, rows, len(offsets)),
        out_shape=shapes,
        in_specs=[smem()] * (2 + len(offsets)) + [vmem()] * 2 + [hbm()] * 4,
        out_specs=[vmem()] * len(shapes),
        scratch_shapes=[pltpu.SemaphoreType.DMA((4,))],
        compiler_params=params(),
    )(source_cell, wavelet, *offsets, receiver_cell, traces, *stay(*fields))


def advance(now, at, before, before_at, courant, courant_at, inject, inject_at, runs, step, along_z, along_y, write):
    size_y, size_z = now.shape[-2:]
    pieces = [now[at + first : at + first + count].reshape(count * size_y, size_z) for first, count in runs]
    value = pieces[0] if len(pieces) == 1 else jnp.concatenate(pieces, axis=0)
    high = value.astype(jnp.bfloat16)
    low = (value - high.astype(jnp.float32)).astype(jnp.bfloat16)
    dot = functools.partial(jnp.dot, preferred_element_type=jnp.float32)
    sides = dot(high, along_z) + dot(low, along_z)
    sides = sides + dot(along_y, jnp.concatenate([high, low], axis=0))
    lane = lax.broadcasted_iota(jnp.int32, (size_y, LANES), 1)
    for i, plane in enumerate(first + j for first, count in runs for j in range(count)):
        here = at + plane
        own = now[here]
        total = sides[i * size_y : (i + 1) * size_y] + OWN * own
        for distance, tap in enumerate(TAPS, 1):
            pair = now[here + distance] + now[here - distance]
            total = total + (pair if tap == 1.0 else tap * pair)
        new = (own + own) - before[before_at + plane] + courant[courant_at + plane] * total
        spot = pltpu.roll(inject[inject_at + plane], (INJECT_Z - step) % LANES, 1)
        near = new[:, :LANES] + jnp.where(lane == INJECT_Z, spot, 0.0)
        write(i, plane, jnp.concatenate([near, new[:, LANES:]], axis=1))


def chunks(start, stop):
    return [[(at, CHUNK)] for at in range(start, stop, CHUNK)]


def first_kernel(rows, last, width, now, before, courant, even, odd, inject, along_z, along_y, fresh, held, even_edge, odd_edge, scaled):
    even_at, odd_at = halo_starts(rows, REACH)
    inside = REACH if last else 0
    scaled[inside : inside + rows] = SCALE * courant[...]
    if last:
        scaled[pl.ds(even_at, REACH)] = SCALE * even[2]
        scaled[pl.ds(odd_at, REACH)] = SCALE * odd[2]
    z_band, y_band = along_z[...], along_y[...]
    for kind in range(2):
        field = held.at[kind]
        field[REACH : REACH + rows] = now[kind]
        field[pl.ds(even_at, REACH)] = even[kind]
        field[pl.ds(odd_at, REACH)] = odd[kind]

        def write(i, plane, new, kind=kind):
            fresh[kind, plane] = new

        for runs in chunks(0, rows):
            advance(field, REACH, before.at[kind], 0, scaled, inside, inject.at[kind], REACH, runs, 0, z_band, y_band, write)
    send(rows, width, fresh, even_edge, odd_edge)


def send(rows, width, fresh, even_edge, odd_edge):
    even_from, odd_from = edge_starts(rows, width)
    even_edge[...] = fresh[:, pl.ds(even_from, width)]
    odd_edge[...] = fresh[:, pl.ds(odd_from, width)]


def first_round(group, groups, width, now, before, courant, halos, inject, along_z, along_y):
    rows, size_y, size_z = now.shape[1:]
    last = group == groups - 1
    edge = struct((2, width, size_y, size_z))
    shapes = [struct(now.shape), struct((2, rows + 2 * REACH, size_y, size_z)), edge, edge]
    scratch = []
    if last:
        shapes.append(struct((rows + 2 * REACH, size_y, size_z)))
    else:
        scratch.append(pltpu.VMEM((rows, size_y, size_z), jnp.float32))
    return pl.pallas_call(
        functools.partial(first_kernel, rows, last, width),
        out_shape=shapes,
        in_specs=[vmem()] * 8,
        out_specs=[vmem()] * len(shapes),
        scratch_shapes=scratch,
        compiler_params=params(),
    )(now, before, courant, *halos, inject, along_z, along_y)


def pair_kernel(rows, step, width, now, before, even, odd, courant, inject, along_z, along_y, fresh, held, even_edge, odd_edge, wide):
    reach = 2 * REACH
    even_at, odd_at = halo_starts(rows, reach)
    z_band, y_band = along_z[...], along_y[...]
    for kind in range(2):
        field = wide.at[kind]
        field[reach : reach + rows] = now[kind]
        field[pl.ds(even_at, reach)] = even[kind]
        field[pl.ds(odd_at, reach)] = odd[kind]
        middle = held.at[kind]

        def write_middle(i, plane, new, kind=kind):
            held[kind, REACH + plane] = new

        def write(i, plane, new, kind=kind):
            fresh[kind, plane] = new

        for runs in chunks(-REACH, rows + REACH):
            advance(field, reach, before.at[kind], REACH, courant, REACH, inject.at[kind], REACH, runs, step, z_band, y_band, write_middle)
        for runs in chunks(0, rows):
            advance(middle, REACH, field, reach, courant, REACH, inject.at[kind], REACH, runs, step + 1, z_band, y_band, write)
    send(rows, width, fresh, even_edge, odd_edge)


def pair_round(step, width, now, before, halos, courant, inject, along_z, along_y):
    rows, size_y, size_z = now.shape[1:]
    edge = struct((2, width, size_y, size_z))
    shapes = [struct(now.shape), struct((2, rows + 2 * REACH, size_y, size_z)), edge, edge]
    return pl.pallas_call(
        functools.partial(pair_kernel, rows, step, width),
        out_shape=shapes,
        in_specs=[vmem()] * 8,
        out_specs=[vmem()] * 4,
        scratch_shapes=[pltpu.VMEM((2, rows + 4 * REACH, size_y, size_z), jnp.float32)],
        compiler_params=params(),
    )(now, before, *halos, courant, inject, along_z, along_y)


def inner_kernel(group, rows, step, now, before, courant, inject, along_z, along_y, *refs):
    final = refs[-1]
    z_band, y_band = along_z[...], along_y[...]
    for kind in range(2):

        def write(i, plane, new, place=2 * group + kind):
            final[place, plane - REACH] = new

        for runs in chunks(REACH, rows - REACH):
            advance(now.at[kind], 0, before.at[kind], REACH, courant, REACH, inject.at[kind], REACH, runs, step, z_band, y_band, write)


def inner_round(group, groups, step, now, before, courant, inject, along_z, along_y, final):
    rows, size_y, size_z = now.shape[1:]
    return pl.pallas_call(
        functools.partial(inner_kernel, group, rows, step),
        out_shape=struct((2 * groups, rows - 2 * REACH, size_y, size_z)),
        in_specs=[vmem()] * (6 + len(final)),
        out_specs=vmem(),
        input_output_aliases={6: 0} if final else {},
        compiler_params=params(),
    )(now, before, courant, inject, along_z, along_y, *final)


def outer_kernel(rows, step, now, before, even, odd, courant, inject, along_z, along_y, final, wide):
    even_at, odd_at = halo_starts(rows, REACH)
    z_band, y_band = along_z[...], along_y[...]
    for kind in range(2):
        field = wide.at[kind]
        field[REACH : REACH + rows] = now[kind]
        field[pl.ds(even_at, REACH)] = even[kind]
        field[pl.ds(odd_at, REACH)] = odd[kind]

        def write(i, plane, new, kind=kind):
            final[kind, i] = new

        runs = [(0, REACH), (rows - REACH, REACH)]
        advance(field, REACH, before.at[kind], REACH, courant, REACH, inject.at[kind], REACH, runs, step, z_band, y_band, write)


def outer_round(step, now, before, halos, courant, inject, along_z, along_y):
    rows, size_y, size_z = now.shape[1:]
    return pl.pallas_call(
        functools.partial(outer_kernel, rows, step),
        out_shape=struct((2, 2 * REACH, size_y, size_z)),
        in_specs=[vmem()] * 8,
        out_specs=vmem(),
        scratch_shapes=[pltpu.VMEM((2, rows + 2 * REACH, size_y, size_z), jnp.float32)],
        compiler_params=params(),
    )(now, before, *halos, courant, inject, along_z, along_y)


def shifted(plane, amount):
    size_y = plane.shape[0]
    if amount == 0:
        return plane
    if abs(amount) >= size_y:
        return jnp.zeros_like(plane)
    row = lax.broadcasted_iota(jnp.int32, plane.shape, 0)
    inside = (row >= amount) if amount > 0 else (row < size_y + amount)
    return jnp.where(inside, pltpu.roll(plane, amount % size_y, 0), 0.0)


def partial_image(ahead, lags, fields, image, others=()):
    count = lags.shape[0]
    half_span = count // 2
    slots, rows = image.shape[:2]
    here = lax.axis_index("shot")
    pairs = lax.axis_size("shot") // 2
    owner = 2 * lax.rem(lax.div(here, 2) + ahead, pairs) + lax.rem(here, 2)

    def one_slot(slot, carry):
        index = jnp.max(lags[pl.ds(owner * slots + slot, 1), :])
        for lag_index in range(count):
            lag = lag_index - half_span

            @pl.when(index == lag_index)
            def _(lag=lag):
                def one_plane(x, carry):
                    total = None
                    for field in fields:
                        for source in range(0, field.shape[0], 2):
                            term = field[source + 1, x] * shifted(field[source, x], 2 * lag)
                            total = term if total is None else total + term
                    total = shifted(total, -lag)
                    for other in others:
                        total = total + other[slot, x]
                    image[slot, x] = total
                    return carry

                lax.fori_loop(0, rows, one_plane, 0, unroll=4)

        return carry

    lax.fori_loop(0, slots, one_slot, 0)


def image_kernel(ahead, lags, *refs):
    partial_image(ahead, lags, refs[:-1], refs[-1])


def image_part(ahead, slots, lags, fields):
    _, rows, size_y, size_z = fields[0].shape
    return pl.pallas_call(
        functools.partial(image_kernel, ahead),
        out_shape=struct((slots, rows, size_y, size_z)),
        in_specs=[vmem()] * (1 + len(fields)),
        out_specs=vmem(),
        compiler_params=params(),
    )(lags, *fields)


def inner_image_kernel(groups, rows, lags, *refs):
    inner_fields, outer_fields, others = refs[:2], refs[2 : 2 + 2 * groups], refs[2 + 2 * groups : -6]
    image, source_out, receiver_out, outer, inner, sem = refs[-6:]
    copies = []
    for group in range(groups):
        for kind, out in enumerate((source_out, receiver_out)):
            pieces = (
                (inner_fields[0].at[2 * group + kind], REACH, rows - 2 * REACH),
                (outer_fields[group].at[kind, pl.ds(0, REACH)], 0, REACH),
                (outer_fields[group].at[kind, pl.ds(REACH, REACH)], rows - REACH, REACH),
            )
            for piece, first, count in pieces:
                copies.append(pltpu.make_async_copy(piece, out.at[group, pl.ds(first, count)], sem.at[len(copies)]))
                copies[-1].start()
    partial_image(0, lags, inner_fields, inner, others)
    copies.append(pltpu.make_async_copy(inner, image.at[:, pl.ds(REACH, rows - 2 * REACH)], sem.at[len(copies)]))
    copies[-1].start()
    partial_image(0, lags, outer_fields, outer)
    for copy in copies:
        copy.wait()


def inner_image(slots, inner, outer, others, lags):
    places, inner_rows, size_y, size_z = inner[0].shape
    groups, rows = places // 2, inner_rows + 2 * REACH
    whole = struct((groups, rows, size_y, size_z))
    return pl.pallas_call(
        functools.partial(inner_image_kernel, groups, rows),
        out_shape=[struct((slots, rows, size_y, size_z)), whole, whole, struct((slots, 2 * REACH, size_y, size_z))],
        in_specs=[vmem()] * (1 + len(inner) + len(outer) + len(others)),
        out_specs=[hbm()] * 3 + [vmem()],
        scratch_shapes=[pltpu.VMEM((slots, inner_rows, size_y, size_z), jnp.float32), pltpu.SemaphoreType.DMA((3 * places + 1,))],
        compiler_params=params(),
        name="image_inner",
    )(lags, *inner, *outer, *others)


def outer_image_kernel(rows, *refs):
    own, others = refs[0], refs[1:-4]
    image, outer, sem = refs[-3:]
    copies = []
    for side, first in enumerate((0, rows - REACH)):
        planes = pl.ds(side * REACH, REACH)
        total = own[:, planes]
        for other in others:
            total = total + other[:, planes]
        outer[:, planes] = total
        copies.append(pltpu.make_async_copy(outer.at[:, planes], image.at[:, pl.ds(first, REACH)], sem.at[side]))
        copies[side].start()
    for copy in copies:
        copy.wait()


def outer_image(image, own, others):
    return pl.pallas_call(
        functools.partial(outer_image_kernel, image.shape[1]),
        out_shape=struct(image.shape),
        in_specs=[vmem()] * (1 + len(others)) + [hbm()],
        out_specs=hbm(),
        scratch_shapes=[pltpu.VMEM(own.shape, jnp.float32), pltpu.SemaphoreType.DMA((2,))],
        input_output_aliases={1 + len(others): 0},
        compiler_params=params(),
        name="image_outer",
    )(own, *others, image)


def program(source_now, source_prev, receiver_now, receiver_prev, courant_sq, source_cell, wavelet, receiver_cell, traces, offset_perm):
    groups, _, _, _ = source_now.shape
    steps = wavelet.shape[0]
    shot_devices = lax.axis_size("shot")
    slots = offset_perm.shape[0] // shot_devices
    everyone = range(groups)

    edges = pack(source_now, receiver_now, courant_sq)
    given = [trade(edges[2 * g], edges[2 * g + 1]) for g in everyone]
    fields = (source_now, receiver_now, source_prev, receiver_prev)
    inject, now, before = [None] * groups, [None] * groups, [None] * groups
    for g in everyone:
        inject[g], now[g], before[g], *tables = prepare(g, source_cell, wavelet, offset_perm, receiver_cell, traces, fields)
        if g == 0:
            along_z, along_y = tables[:2]
    lags = tables[-1]

    halos = [None] * groups
    for g in everyone:
        result = first_round(g, groups, 2 * REACH, now[g], before[g], courant_sq, given[g], inject[g], along_z, along_y)
        now[g], before[g] = result[:2]
        halos[g] = trade(*result[2:4])
    courant = result[4]
    final = ()
    for step in range(1, steps - 1, 2):
        last = step + 2 >= steps - 1
        for g in everyone:
            now[g], before[g], even, odd = pair_round(step, REACH if last else 2 * REACH, now[g], before[g], halos[g], courant, inject[g], along_z, along_y)
            halos[g] = trade(even, odd)
            if last:
                final = (inner_round(g, groups, steps - 1, now[g], before[g], courant, inject[g], along_z, along_y, final),)

    swap = [(i, i ^ 1) for i in range(shot_devices)]
    pairs = shot_devices // 2

    def traded(own):
        return lax.ppermute(own, "shot", swap)

    def part_sums(fields):
        parts = [image_part(ahead, slots, lags, fields) for ahead in range(1, pairs)]
        sums = []
        for ahead, part in enumerate(parts, 1):
            route = [(2 * p + c, 2 * ((p + ahead) % pairs) + c) for p in range(pairs) for c in range(2)]
            sums.append(lax.ppermute(part, "shot", route))
        return sums

    inner = (*final, traded(*final))
    inner_sums = part_sums(inner)
    own, other = [], []
    for g in everyone:
        own.append(outer_round(steps - 1, now[g], before[g], halos[g], courant, inject[g], along_z, along_y))
        other.append(traded(own[g]))
    outer = (*own, *other)
    outer_sums = part_sums(outer)
    image, source_final, receiver_final, part = inner_image(slots, inner, outer, inner_sums, lags)
    image = outer_image(image, part, outer_sums)
    return image, source_final, receiver_final


def solution(mesh):
    shots = ("runs", "shot")
    in_specs = (
        P(shots, "slab", None, None),
        P(shots, "slab", None, None),
        P(shots, "slab", None, None),
        P(shots, "slab", None, None),
        P(("runs", "slab"), None, None),
        P(shots),
        P(None, shots),
        P(shots, None),
        P(None, shots, None),
        P("runs"),
    )
    out_specs = (P(shots, "slab", None, None),) * 3
    return jax.shard_map(program, mesh=mesh, in_specs=in_specs, out_specs=out_specs, check_vma=False)
```
